512 devices in a mesh: ctx: 32 (over x, y, core), head: 16 (over z).
Axes of the slice: x: 4, y: 4, z: 16, core: 2. Of those that a mesh axis runs over, the one named last changes fastest.
Arguments:
- x_in: bfloat16 [49152, 8192], P(('ctx', 'head')), may hold values from -6 to 6
- dt_raw: bfloat16 [49152, 128], P(('ctx', 'head')), may hold values from -3 to 3
- bc_in: bfloat16 [49152, 256], P(('ctx', 'head')), may hold values from -6 to 6
- z_in: bfloat16 [49152, 8192], P(('ctx', 'head')), may hold values from -6 to 6
- conv_x: float32 [4, 8192], P(None, 'head'), may hold values from -3 to 3
- bias_x: float32 [8192], P('head'), may hold values from -3 to 3
- conv_bc: float32 [4, 256], replicated, may hold values from -3 to 3
- bias_bc: float32 [256], replicated, may hold values from -3 to 3
- dt_bias: float32 [128], P('head'), may hold values from -0.5 to 0.5
- a_log: float32 [128], P('head'), may hold values from -16 to -2
- d_skip: float32 [128], P('head'), may hold values from 0.5 to 1.5
- norm_gain: float32 [8192], replicated, may hold values from 0.5 to 1.5
Outputs:
- mixed: bfloat16 [49152, 8192], P(('ctx', 'head'))
The draws below stay inside these ranges and needn't reach their ends.
All inputs are finite; a program needn't handle non-finite values.
Results may differ from the reference program's by a relative error of at most 0.0015.
The reference program's roundings to bfloat16 on the way count: a program that leaves them out, or rounds other values in their place, can miss the bound.
Values may be sent and summed in bfloat16 or wider, within the bound.
No kernel may reach another device: no remote copies, remote signals or barrier semaphores. Data moves between devices by JAX's collectives and lax.ppermute only.
A program may use at most 64 MiB of HBM per device.

```python
import jax
import jax.numpy as jnp
from jax import lax

NHEADS = 128
HEADDIM = 64
STATE = 128
BLOCK = 256
INNER = 8192
TOKENS = 49152


def draw_a_log(key, part):
    key_pick = jax.random.fold_in(key, 11)
    key_slow = jax.random.fold_in(key, 12)
    key_fast = jax.random.fold_in(key, 13)
    quick = jax.random.bernoulli(key_pick, 0.5, (NHEADS,))
    slow_rate = jax.random.uniform(key_slow, (NHEADS,), jnp.float32, 0.3, 1.0) / TOKENS
    fast_rate = jnp.exp(jax.random.uniform(key_fast, (NHEADS,), jnp.float32, jnp.log(1.0 / 40.0), jnp.log(1.0 / 15.0)))
    return jnp.log(jnp.where(quick, fast_rate, slow_rate)).astype(jnp.float32)


def levels(rng, extent, pieces, low, high):
    factor_of, own = 1.0, jax.random.fold_in(rng, 6)
    for dim, blocks in pieces:
        heights = jnp.exp(jax.random.uniform(jax.random.fold_in(own, dim), (blocks,), jnp.float32, low / len(pieces), high / len(pieces)))
        factor_of = factor_of * jnp.repeat(heights, extent[dim] // blocks).reshape([-1 if axis == dim else 1 for axis in range(len(extent))])
    return factor_of


def normal_values(own_key, extent, scale, most, shards=(), dtype=jnp.bfloat16):
    array = scale * jax.random.normal(own_key, extent, jnp.float32)
    if shards:
        array = array * levels(own_key, extent, shards, -0.22, 0.18)
    return jnp.clip(array, -most, most).astype(dtype)


def setup_inputs(seed: int = 0) -> dict:
    seeds = jax.random.split(jax.random.key(seed), 13)
    x_in = normal_values(seeds[0], (TOKENS, INNER), 1.0, 6.0, ((0, 512),))
    dt_raw = normal_values(seeds[1], (TOKENS, NHEADS), 0.5, 3.0, ((0, 512),))
    bc_in = normal_values(seeds[2], (TOKENS, 2 * STATE), 1.0, 6.0, ((0, 512),))
    z_in = normal_values(seeds[3], (TOKENS, INNER), 1.0, 6.0, ((0, 512),))
    conv_x = normal_values(seeds[4], (4, INNER), 0.5, 3.0, ((1, 16),), jnp.float32)
    bias_x = normal_values(seeds[5], (INNER,), 0.5, 3.0, ((0, 16),), jnp.float32)
    conv_bc = normal_values(seeds[6], (4, 2 * STATE), 0.5, 3.0, (), jnp.float32)
    bias_bc = normal_values(seeds[7], (2 * STATE,), 0.5, 3.0, (), jnp.float32)
    dt_bias = jnp.clip(jax.random.uniform(seeds[8], (NHEADS,), jnp.float32, -0.5, 0.5) * levels(seeds[8], (NHEADS,), ((0, 16),), -0.4, 0.0), -0.5, 0.5)
    a_log = draw_a_log(jax.random.fold_in(seeds[12], 71), 0)
    d_skip = jnp.clip(0.5 + 1.0 * jax.random.uniform(seeds[10], (NHEADS,), jnp.float32) ** levels(seeds[10], (NHEADS,), ((0, 16),), -0.2, 0.2), 0.5, 1.5)
    norm_gain = jnp.clip(1.0 + 0.1 * jax.random.normal(seeds[11], (INNER,), jnp.float32), 0.5, 1.5)
    return {"x_in": x_in, "dt_raw": dt_raw, "bc_in": bc_in, "z_in": z_in, "conv_x": conv_x, "bias_x": bias_x, "conv_bc": conv_bc, "bias_bc": bias_bc, "dt_bias": dt_bias, "a_log": a_log, "d_skip": d_skip, "norm_gain": norm_gain}


def causal_conv(values, taps, offset):
    widths = values.shape[1]
    padded = jnp.concatenate([jnp.zeros((3, widths), jnp.float32), values.astype(jnp.float32)], 0)
    summed = offset[None, :] + taps[0] * padded[0:-3] + taps[1] * padded[1:-2] + taps[2] * padded[2:-1] + taps[3] * padded[3:]
    return jax.nn.silu(summed).astype(jnp.bfloat16)

def reference(x_in, dt_raw, bc_in, z_in, conv_x, bias_x, conv_bc, bias_bc, dt_bias, a_log, d_skip, norm_gain):
    x_conv = causal_conv(x_in, conv_x, bias_x)
    bc_conv = causal_conv(bc_in, conv_bc, bias_bc)
    b_mat = bc_conv[:, :STATE]
    c_mat = bc_conv[:, STATE:]
    step_size = jax.nn.softplus(dt_raw.astype(jnp.float32) + dt_bias[None, :])
    log_decay = step_size * (-jnp.exp(a_log))[None, :]
    nblk = TOKENS // BLOCK
    x_blk = x_conv.reshape(nblk, BLOCK, NHEADS, HEADDIM)
    b_blk = b_mat.reshape(nblk, BLOCK, STATE)
    c_blk = c_mat.reshape(nblk, BLOCK, STATE)
    dt_blk = step_size.reshape(nblk, BLOCK, NHEADS)
    la_blk = log_decay.reshape(nblk, BLOCK, NHEADS)
    lower = jnp.arange(BLOCK)[:, None] >= jnp.arange(BLOCK)[None, :]

    def advance(h_state, inputs):
        x_now, b_now, c_now, dt_now, la_now = inputs
        cum_sum = jnp.cumsum(la_now, axis=0)
        scores = jnp.dot(c_now, b_now.T, preferred_element_type=jnp.float32)
        cum_t = cum_sum.T
        spread = jnp.exp(jnp.where(lower[None], cum_t[:, :, None] - cum_t[:, None, :], -1e+30))
        m_mat = (scores[None] * spread * dt_now.T[:, None, :]).astype(jnp.bfloat16)
        y_diag = jnp.einsum('hts,shp->thp', m_mat.astype(jnp.float32), x_now.astype(jnp.float32))
        h_bf = h_state.astype(jnp.bfloat16)
        y_off = jnp.einsum('tn,hnp->thp', c_now.astype(jnp.float32), h_bf.astype(jnp.float32)) * jnp.exp(cum_sum)[:, :, None]
        y_out = (y_diag + y_off + d_skip[None, :, None] * x_now.astype(jnp.float32)).astype(jnp.bfloat16)
        weight = jnp.exp(cum_sum[-1][None, :] - cum_sum) * dt_now
        b_weighted = (b_now.astype(jnp.float32)[:, None, :] * weight[:, :, None]).astype(jnp.bfloat16)
        st_new = jnp.einsum('qhn,qhp->hnp', b_weighted.astype(jnp.float32), x_now.astype(jnp.float32))
        h_next = h_state * jnp.exp(cum_sum[-1])[:, None, None] + st_new
        return (h_next, y_out)
    start = jnp.zeros((NHEADS, STATE, HEADDIM), jnp.float32)
    _, y_all = lax.scan(advance, start, (x_blk, b_blk, c_blk, dt_blk, la_blk))
    y_flat = y_all.reshape(TOKENS, INNER)
    gated = y_flat.astype(jnp.float32) * jax.nn.silu(z_in.astype(jnp.float32))
    mean_sq = lax.optimization_barrier(jnp.mean(gated * gated, axis=-1, keepdims=True))
    return (gated * lax.rsqrt(mean_sq + 1e-05) * norm_gain[None, :]).astype(jnp.bfloat16)
```

```python
import jax
import jax.numpy as jnp
from jax import lax
from jax.experimental import pallas as pl
from jax.experimental.pallas import tpu as pltpu
from jax.sharding import PartitionSpec as P

BLOCK = 256
STATE = 128
WIDTH = 64
HEADS = 4
LANES = HEADS * WIDTH
CHUNKS = 2
RIM = 16
F32 = jnp.float32
BF16 = jnp.bfloat16


def silu(u):
    return u / (1.0 + jnp.exp(-u))


def causal_conv(before, rows, taps, offset):
    count = rows.shape[0]
    padded = jnp.concatenate([before, rows], 0).astype(F32)
    summed = offset + taps[0:1] * padded[RIM - 3 : RIM - 3 + count]
    summed = summed + taps[1:2] * padded[RIM - 2 : RIM - 2 + count]
    summed = summed + taps[2:3] * padded[RIM - 1 : RIM - 1 + count]
    summed = summed + taps[3:4] * padded[RIM : RIM + count]
    return silu(summed).astype(BF16)


def prep_kernel(g_ref, rim_ref, taps_ref, bias_ref, pick_ref, par_ref, c_ref, bt_ref, rows_ref, cols_ref, carry):
    @pl.when(pl.program_id(0) == 0)
    def _():
        carry[...] = rim_ref[...]

    raw = g_ref[:, : 2 * STATE]
    bcc = causal_conv(carry[...], raw, taps_ref[...], bias_ref[...])
    carry[...] = raw[BLOCK - RIM :]
    c_ref[...] = bcc[:, STATE:]
    bt_ref[...] = bcc[:, :STATE].astype(F32).T.astype(BF16)
    dt_raw = lax.dot_general(
        pick_ref[...], g_ref[:, 2 * STATE :], (((1,), (1,)), ((), ())), preferred_element_type=F32
    )
    shifted = dt_raw + par_ref[0]
    dt = jnp.maximum(shifted, 0.0) + jnp.log1p(jnp.exp(-jnp.abs(shifted)))
    cs = dt * -jnp.exp(par_ref[1])
    lane = lax.broadcasted_iota(jnp.int32, cs.shape, 1)
    step = 1
    while step < BLOCK:
        cs = cs + jnp.where(lane >= step, pltpu.roll(cs, step, 1), 0.0)
        step *= 2
    tot = cs[:, BLOCK - 1 :]
    rows_ref[0:8] = cs
    rows_ref[8:16] = dt
    rows_ref[16:24] = jnp.exp(tot - cs) * dt
    cols_ref[...] = jnp.concatenate([cs, jnp.exp(cs)], 0).T


def lane_pair(first, second, shape):
    lane = lax.broadcasted_iota(jnp.int32, shape, 1)
    return jnp.where(lane < WIDTH, first, second)


def state_kernel(chunk, x_ref, rim_ref, taps_ref, bias_ref, bt_ref, rows_ref, xc_ref, local_ref, sum_ref, carry):
    @pl.when(pl.program_id(0) == 0)
    def _():
        carry[...] = rim_ref[...]
        sum_ref[...] = jnp.zeros_like(sum_ref)

    raw = x_ref[...]
    xc = causal_conv(carry[...], raw, taps_ref[...], bias_ref[...])
    carry[...] = raw[BLOCK - RIM :]
    xc_ref[...] = xc
    local_ref[0] = sum_ref[...]
    bt = bt_ref[...].astype(F32)
    for pair in range(HEADS // 2):
        cols = slice(2 * WIDTH * pair, 2 * WIDTH * (pair + 1))
        parts, tots = [], []
        for h in (HEADS * chunk + 2 * pair, HEADS * chunk + 2 * pair + 1):
            bw = (bt * rows_ref[16 + h : 17 + h]).astype(BF16)
            parts.append(jnp.dot(bw, xc[:, cols], preferred_element_type=F32))
            tots.append(rows_ref[h : h + 1, BLOCK - 1 :])
        tot = lane_pair(tots[0], tots[1], (1, 2 * WIDTH))
        st = lane_pair(parts[0], parts[1], (STATE, 2 * WIDTH))
        sum_ref[:STATE, cols] = sum_ref[:STATE, cols] * jnp.exp(tot) + st
        sum_ref[STATE:, cols] = sum_ref[STATE:, cols] + tot


def diag_kernel(chunk, xc_ref, c_ref, bt_ref, rows_ref, cols_ref, skip_ref, y_ref):
    half = BLOCK // 2
    xc = xc_ref[...]
    scores = jnp.dot(c_ref[...], bt_ref[...], preferred_element_type=F32)
    for low, width in ((0, half), (half, BLOCK)):
        part = scores[low : low + half, :width]
        row = lax.broadcasted_iota(jnp.int32, (half, width), 0) + low
        col = lax.broadcasted_iota(jnp.int32, (half, width), 1)
        keep = row >= col
        for pair in range(HEADS // 2):
            cols = slice(2 * WIDTH * pair, 2 * WIDTH * (pair + 1))
            outs = []
            for h in (HEADS * chunk + 2 * pair, HEADS * chunk + 2 * pair + 1):
                gap = cols_ref[low : low + half, h : h + 1] - rows_ref[h : h + 1, :width]
                spread = jnp.exp(jnp.where(keep, gap, -1e30))
                m = (part * spread * rows_ref[8 + h : 9 + h, :width]).astype(BF16)
                outs.append(jnp.dot(m, xc[:width, cols], preferred_element_type=F32))
            y = lane_pair(outs[0], outs[1], (half, 2 * WIDTH))
            y_ref[low : low + half, cols] = (
                y + skip_ref[:, cols] * xc[low : low + half, cols].astype(F32)
            )


def join_kernel(chunk, yd_ref, c_ref, cols_ref, local_ref, in_ref, y_ref):
    hb = (in_ref[:STATE] * jnp.exp(local_ref[0, STATE : STATE + 1]) + local_ref[0, :STATE]).astype(BF16)
    off = jnp.dot(c_ref[...], hb, preferred_element_type=F32)
    for pair in range(HEADS // 2):
        cols = slice(2 * WIDTH * pair, 2 * WIDTH * (pair + 1))
        h = 8 + HEADS * chunk + 2 * pair
        scale = lane_pair(cols_ref[:, h : h + 1], cols_ref[:, h + 1 : h + 2], (BLOCK, 2 * WIDTH))
        y_ref[:, cols] = (yd_ref[:, cols] + off[:, cols] * scale).astype(BF16)


def gate_kernel(y_ref, z_ref, gated_ref, sq_ref):
    total = jnp.zeros(sq_ref.shape, F32)
    for g in range(y_ref.shape[0]):
        at = slice(CHUNKS * LANES * g, CHUNKS * LANES * g + LANES)
        gated = y_ref[g].astype(F32) * silu(z_ref[:, at].astype(F32))
        gated_ref[g] = gated
        sq = gated * gated
        total = total + sq[:, :128] + sq[:, 128:]
    sq_ref[...] = total


def norm_kernel(y_ref, z_ref, gated_ref, sq_ref, gain_ref, out_ref, late):
    groups = y_ref.shape[0]
    total = sq_ref[...]
    for g in range(groups):
        at = slice(CHUNKS * LANES * g + LANES, CHUNKS * LANES * (g + 1))
        gated = y_ref[g].astype(F32) * silu(z_ref[:, at].astype(F32))
        late[g] = gated
        sq = gated * gated
        total = total + sq[:, :128] + sq[:, 128:]
    mean = jnp.sum(total, axis=1, keepdims=True) * (1.0 / (groups * CHUNKS * LANES))
    scale = lax.rsqrt(mean + 1e-05)
    for g in range(groups):
        at = slice(CHUNKS * LANES * g, CHUNKS * LANES * g + LANES)
        out_ref[:, at] = (gated_ref[g] * scale * gain_ref[:, at]).astype(BF16)
        at = slice(CHUNKS * LANES * g + LANES, CHUNKS * LANES * (g + 1))
        out_ref[:, at] = (late[g] * scale * gain_ref[:, at]).astype(BF16)


def shift(value, axis, by):
    count = lax.axis_size(axis)
    return lax.ppermute(value, axis, [(i, i + by) for i in range(count - by)])


def combine(earlier, later):
    state = earlier[:STATE] * jnp.exp(later[STATE : STATE + 1]) + later[:STATE]
    return jnp.concatenate([state, earlier[STATE:] + later[STATE:]], 0)


def entering(summary, axis):
    reach, window, before = 1, summary, None
    while reach < lax.axis_size(axis):
        got = shift(window, axis, reach)
        before = got if before is None else combine(got, before)
        if 2 * reach < lax.axis_size(axis):
            window = combine(got, window)
        reach *= 2
    return before


def full(shape):
    return pl.BlockSpec(shape, lambda k: tuple(0 for _ in shape))


def rows_of(width):
    return pl.BlockSpec((BLOCK, width), lambda k: (k, 0))


def lanes_of(height):
    return pl.BlockSpec((height, BLOCK), lambda k: (0, k))


PARAMS = pltpu.CompilerParams(dimension_semantics=("arbitrary",), vmem_limit_bytes=40 << 20)


def per_device(
    x_in, dt_raw, bc_in, z_in, conv_x, bias_x, conv_bc, bias_bc, dt_bias, a_log, d_skip, norm_gain
):
    groups = lax.axis_size("head")
    rows = x_in.shape[0]
    seg = rows * groups
    nblk = seg // BLOCK
    heads = dt_bias.shape[0]
    x_parts = x_in.reshape(rows, groups, CHUNKS, LANES)

    def to_groups(chunk):
        part = lax.all_to_all(x_parts[:, :, chunk], "head", 1, 1, tiled=True)
        return part.transpose(1, 0, 2).reshape(seg, LANES)

    def to_tokens(value):
        part = value.reshape(groups, rows, LANES).transpose(1, 0, 2)
        return lax.all_to_all(part, "head", 1, 1, tiled=True).transpose(1, 0, 2)

    gathered = lax.all_gather(jnp.concatenate([bc_in, dt_raw], 1), "head", axis=0, tiled=True)
    x_seg = [to_groups(j) for j in range(CHUNKS)]

    pick = (
        jnp.arange(groups * heads)[None, :] == jnp.arange(heads)[:, None] + heads * lax.axis_index("head")
    ).astype(BF16)
    par = jnp.stack([dt_bias, a_log])[:, :, None]
    par = jnp.broadcast_to(par, (2, heads, BLOCK))
    bc_rim = shift(gathered[seg - RIM :, : 2 * STATE], "ctx", 1)
    c_mat, b_t, row_tab, col_tab = pl.pallas_call(
        prep_kernel,
        grid=(nblk,),
        in_specs=[
            rows_of(gathered.shape[1]),
            full((RIM, 2 * STATE)),
            full((4, 2 * STATE)),
            full((1, 2 * STATE)),
            full(pick.shape),
            full(par.shape),
        ],
        out_specs=[rows_of(STATE), lanes_of(STATE), lanes_of(3 * heads), rows_of(2 * heads)],
        out_shape=[
            jax.ShapeDtypeStruct((seg, STATE), BF16),
            jax.ShapeDtypeStruct((STATE, seg), BF16),
            jax.ShapeDtypeStruct((3 * heads, seg), F32),
            jax.ShapeDtypeStruct((seg, 2 * heads), F32),
        ],
        scratch_shapes=[pltpu.VMEM((RIM, 2 * STATE), BF16)],
        compiler_params=PARAMS,
        name="prep",
    )(gathered, bc_rim, conv_bc, bias_bc[None, :], pick, par)

    y_tok = []
    for j in range(CHUNKS):
        at = slice(LANES * j, LANES * (j + 1))
        rim = shift(x_seg[j][seg - RIM :], "ctx", 1)
        xc, local, summary = pl.pallas_call(
            lambda *refs, j=j: state_kernel(j, *refs),
            grid=(nblk,),
            in_specs=[
                rows_of(LANES),
                full((RIM, LANES)),
                full((4, LANES)),
                full((1, LANES)),
                lanes_of(STATE),
                lanes_of(3 * heads),
            ],
            out_specs=[
                rows_of(LANES),
                pl.BlockSpec((1, STATE + 8, LANES), lambda k: (k, 0, 0)),
                full((STATE + 8, LANES)),
            ],
            out_shape=[
                jax.ShapeDtypeStruct((seg, LANES), BF16),
                jax.ShapeDtypeStruct((nblk, STATE + 8, LANES), F32),
                jax.ShapeDtypeStruct((STATE + 8, LANES), F32),
            ],
            scratch_shapes=[pltpu.VMEM((RIM, LANES), BF16)],
            compiler_params=PARAMS,
            name=f"state{j}",
        )(x_seg[j], rim, conv_x[:, at], bias_x[None, at], b_t, row_tab)
        incoming = entering(summary, "ctx")
        skip = jnp.repeat(d_skip[HEADS * j : HEADS * (j + 1)], WIDTH)[None, :]
        y_diag = pl.pallas_call(
            lambda *refs, j=j: diag_kernel(j, *refs),
            grid=(nblk,),
            in_specs=[
                rows_of(LANES),
                rows_of(STATE),
                lanes_of(STATE),
                lanes_of(3 * heads),
                rows_of(2 * heads),
                full((1, LANES)),
            ],
            out_specs=rows_of(LANES),
            out_shape=jax.ShapeDtypeStruct((seg, LANES), F32),
            compiler_params=PARAMS,
            name=f"diag{j}",
        )(xc, c_mat, b_t, row_tab, col_tab, skip)
        y = pl.pallas_call(
            lambda *refs, j=j: join_kernel(j, *refs),
            grid=(nblk,),
            in_specs=[
                rows_of(LANES),
                rows_of(STATE),
                rows_of(2 * heads),
                pl.BlockSpec((1, STATE + 8, LANES), lambda k: (k, 0, 0)),
                full((STATE + 8, LANES)),
            ],
            out_specs=rows_of(LANES),
            out_shape=jax.ShapeDtypeStruct((seg, LANES), BF16),
            compiler_params=PARAMS,
            name=f"join{j}",
        )(y_diag, c_mat, col_tab, local, incoming)
        y_tok.append(to_tokens(y))

    gated, squares = pl.pallas_call(
        gate_kernel,
        out_shape=[
            jax.ShapeDtypeStruct((groups, rows, LANES), F32),
            jax.ShapeDtypeStruct((rows, 128), F32),
        ],
        compiler_params=pltpu.CompilerParams(vmem_limit_bytes=40 << 20),
        name="gate",
    )(y_tok[0], z_in)
    return pl.pallas_call(
        norm_kernel,
        out_shape=jax.ShapeDtypeStruct(z_in.shape, BF16),
        scratch_shapes=[pltpu.VMEM((groups, rows, LANES), F32)],
        compiler_params=pltpu.CompilerParams(vmem_limit_bytes=40 << 20),
        name="norm",
    )(y_tok[1], z_in, gated, squares, norm_gain[None, :])


def solution(mesh):
    token = P(("ctx", "head"), None)
    in_specs = (
        token,
        token,
        token,
        token,
        P(None, "head"),
        P("head"),
        P(),
        P(),
        P("head"),
        P("head"),
        P("head"),
        P(),
    )
    return jax.shard_map(per_device, mesh=mesh, in_specs=in_specs, out_specs=token, check_vma=False)
```

```python
import jax
import jax.numpy as jnp
from jax import lax
from jax.experimental import pallas as pl
from jax.experimental.pallas import tpu as pltpu
from jax.sharding import PartitionSpec as P

BLOCK = 256
STATE = 128
WIDTH = 64
HEADS = 4
LANES = HEADS * WIDTH
CHUNKS = 2
RIM = 16
F32 = jnp.float32
BF16 = jnp.bfloat16


def silu(u):
    return u / (1.0 + jnp.exp(-u))


def causal_conv(before, rows, taps, offset):
    count = rows.shape[0]
    padded = jnp.concatenate([before, rows], 0).astype(F32)
    summed = offset + taps[0:1] * padded[RIM - 3 : RIM - 3 + count]
    summed = summed + taps[1:2] * padded[RIM - 2 : RIM - 2 + count]
    summed = summed + taps[2:3] * padded[RIM - 1 : RIM - 1 + count]
    summed = summed + taps[3:4] * padded[RIM : RIM + count]
    return silu(summed).astype(BF16)


def pack_kernel(chunk, x_ref, *refs):
    out_ref = refs[-1]
    rows = x_ref.shape[0]
    for g in range(out_ref.shape[0]):
        start = LANES * (CHUNKS * g + chunk)
        out_ref[g, :rows] = x_ref[:, start : start + LANES]
    if chunk == 0:
        dt = refs[0][...].astype(F32).T.astype(BF16)
        heads = dt.shape[0] // out_ref.shape[0]
        for g in range(out_ref.shape[0]):
            out_ref[g, rows:, :rows] = dt[heads * g : heads * (g + 1)]
            out_ref[g, rows:, rows:] = jnp.zeros((heads, LANES - rows), BF16)


def prep_kernel(g_ref, rim_ref, taps_ref, bias_ref, dt_ref, par_ref, c_ref, bt_ref, rows_ref, cols_ref, carry):
    @pl.when(pl.program_id(0) == 0)
    def _():
        carry[...] = rim_ref[...]

    raw = g_ref[...]
    bcc = causal_conv(carry[...], raw, taps_ref[...], bias_ref[...])
    carry[...] = raw[BLOCK - RIM :]
    c_ref[...] = bcc[:, STATE:]
    bt_ref[...] = bcc[:, :STATE].astype(F32).T.astype(BF16)
    shifted = dt_ref[...].astype(F32) + par_ref[0]
    dt = jnp.maximum(shifted, 0.0) + jnp.log1p(jnp.exp(-jnp.abs(shifted)))
    cs = dt * -jnp.exp(par_ref[1])
    lane = lax.broadcasted_iota(jnp.int32, cs.shape, 1)
    step = 1
    while step < BLOCK:
        cs = cs + jnp.where(lane >= step, pltpu.roll(cs, step, 1), 0.0)
        step *= 2
    tot = cs[:, BLOCK - 1 :]
    rows_ref[0:8] = cs
    rows_ref[8:16] = dt
    rows_ref[16:24] = jnp.exp(tot - cs) * dt
    cols_ref[...] = jnp.concatenate([cs, jnp.exp(cs)], 0).T


def lane_pair(first, second, shape):
    lane = lax.broadcasted_iota(jnp.int32, shape, 1)
    return jnp.where(lane < WIDTH, first, second)


def state_kernel(chunk, x_ref, rim_ref, taps_ref, bias_ref, bt_ref, rows_ref, xc_ref, local_ref, sum_ref, carry):
    @pl.when(pl.program_id(0) == 0)
    def _():
        carry[...] = rim_ref[...]
        sum_ref[...] = jnp.zeros_like(sum_ref)

    raw = x_ref[...]
    xc = causal_conv(carry[...], raw, taps_ref[...], bias_ref[...])
    carry[...] = raw[BLOCK - RIM :]
    xc_ref[...] = xc
    local_ref[0] = sum_ref[...]
    bt = bt_ref[...].astype(F32)
    for pair in range(HEADS // 2):
        cols = slice(2 * WIDTH * pair, 2 * WIDTH * (pair + 1))
        parts, tots = [], []
        for h in (HEADS * chunk + 2 * pair, HEADS * chunk + 2 * pair + 1):
            bw = (bt * rows_ref[16 + h : 17 + h]).astype(BF16)
            parts.append(jnp.dot(bw, xc[:, cols], preferred_element_type=F32))
            tots.append(rows_ref[h : h + 1, BLOCK - 1 :])
        tot = lane_pair(tots[0], tots[1], (1, 2 * WIDTH))
        st = lane_pair(parts[0], parts[1], (STATE, 2 * WIDTH))
        sum_ref[:STATE, cols] = sum_ref[:STATE, cols] * jnp.exp(tot) + st
        sum_ref[STATE:, cols] = sum_ref[STATE:, cols] + tot


def diag_kernel(chunk, xc_ref, c_ref, bt_ref, rows_ref, cols_ref, skip_ref, y_ref):
    half = BLOCK // 2
    xc = xc_ref[...]
    scores = jnp.dot(c_ref[...], bt_ref[...], preferred_element_type=F32)
    for low, width in ((0, half), (half, BLOCK)):
        part = scores[low : low + half, :width]
        row = lax.broadcasted_iota(jnp.int32, (half, width), 0) + low
        col = lax.broadcasted_iota(jnp.int32, (half, width), 1)
        keep = row >= col
        for pair in range(HEADS // 2):
            cols = slice(2 * WIDTH * pair, 2 * WIDTH * (pair + 1))
            outs = []
            for h in (HEADS * chunk + 2 * pair, HEADS * chunk + 2 * pair + 1):
                gap = cols_ref[low : low + half, h : h + 1] - rows_ref[h : h + 1, :width]
                spread = jnp.exp(jnp.where(keep, gap, -1e30))
                m = (part * spread * rows_ref[8 + h : 9 + h, :width]).astype(BF16)
                outs.append(jnp.dot(m, xc[:width, cols], preferred_element_type=F32))
            y = lane_pair(outs[0], outs[1], (half, 2 * WIDTH))
            y_ref[low : low + half, cols] = (
                y + skip_ref[:, cols] * xc[low : low + half, cols].astype(F32)
            )


def join_kernel(chunk, yd_ref, c_ref, cols_ref, local_ref, near_ref, far_ref, y_ref):
    entry = far_ref[:STATE] * jnp.exp(near_ref[STATE : STATE + 1]) + near_ref[:STATE]
    hb = (entry * jnp.exp(local_ref[0, STATE : STATE + 1]) + local_ref[0, :STATE]).astype(BF16)
    off = jnp.dot(c_ref[...], hb, preferred_element_type=F32)
    for pair in range(HEADS // 2):
        cols = slice(2 * WIDTH * pair, 2 * WIDTH * (pair + 1))
        h = 8 + HEADS * chunk + 2 * pair
        scale = lane_pair(cols_ref[:, h : h + 1], cols_ref[:, h + 1 : h + 2], (BLOCK, 2 * WIDTH))
        y_ref[:, cols] = (yd_ref[:, cols] + off[:, cols] * scale).astype(BF16)


def norm_kernel(first_ref, second_ref, z_ref, gain_ref, out_ref, gated_ref):
    groups = first_ref.shape[0]
    total = jnp.zeros((z_ref.shape[0], 128), F32)
    for g in range(groups):
        for j, y_ref in enumerate((first_ref, second_ref)):
            start = LANES * (CHUNKS * g + j)
            at = slice(start, start + LANES)
            gated = y_ref[g].astype(F32) * silu(z_ref[:, at].astype(F32))
            gated_ref[:, at] = gated
            sq = gated * gated
            total = total + sq[:, :128] + sq[:, 128:]
    mean = jnp.sum(total, axis=1, keepdims=True) * (1.0 / (groups * CHUNKS * LANES))
    out_ref[...] = (gated_ref[...] * lax.rsqrt(mean + 1e-05) * gain_ref[...]).astype(BF16)


def join_pair(earlier, later):
    state = earlier[:STATE] * jnp.exp(later[STATE : STATE + 1]) + later[:STATE]
    return jnp.concatenate([state, earlier[STATE:] + later[STATE:]], 0)


def first_kernel(own_ref, one_ref, two_ref, three_ref, before_ref, window_ref):
    before = join_pair(three_ref[...], join_pair(two_ref[...], one_ref[...]))
    before_ref[...] = before
    window_ref[...] = join_pair(before, own_ref[...])


def second_kernel(own_ref, near_ref, one_ref, two_ref, three_ref, before_ref, window_ref):
    reached = join_pair(three_ref[...], join_pair(two_ref[...], one_ref[...]))
    before_ref[...] = join_pair(reached, near_ref[...])
    window_ref[...] = join_pair(reached, own_ref[...])


def shift(value, axis, by):
    count = lax.axis_size(axis)
    return lax.ppermute(value, axis, [(i, i + by) for i in range(count - by)])


def entering(summary):
    pair = [jax.ShapeDtypeStruct(summary.shape, F32)] * 2
    steps = [shift(summary, "ctx", by) for by in (1, 2, 3)]
    before, window = pl.pallas_call(first_kernel, out_shape=pair, compiler_params=WHOLE, name="first")(summary, *steps)
    steps = [shift(window, "ctx", by) for by in (4, 8, 12)]
    before, window = pl.pallas_call(second_kernel, out_shape=pair, compiler_params=WHOLE, name="second")(window, before, *steps)
    return before, shift(window, "ctx", 16)


def full(shape):
    return pl.BlockSpec(shape, lambda k: tuple(0 for _ in shape))


def rows_of(width):
    return pl.BlockSpec((BLOCK, width), lambda k: (k, 0))


def lanes_of(height):
    return pl.BlockSpec((height, BLOCK), lambda k: (0, k))


WHOLE = pltpu.CompilerParams(vmem_limit_bytes=16 << 20)
PARAMS = pltpu.CompilerParams(dimension_semantics=("arbitrary",), vmem_limit_bytes=16 << 20)


def per_device(
    x_in, dt_raw, bc_in, z_in, conv_x, bias_x, conv_bc, bias_bc, dt_bias, a_log, d_skip, norm_gain
):
    groups = lax.axis_size("head")
    rows = x_in.shape[0]
    seg = rows * groups
    nblk = seg // BLOCK
    heads = dt_bias.shape[0]

    def to_groups(value):
        return lax.all_to_all(value.transpose(1, 0, 2), "head", 1, 1, tiled=True).transpose(1, 0, 2)

    def to_tokens(value):
        part = value.reshape(groups, rows, LANES).transpose(1, 0, 2)
        return lax.all_to_all(part, "head", 1, 1, tiled=True).transpose(1, 0, 2)

    def pack(chunk, height, *values):
        return pl.pallas_call(
            lambda *refs: pack_kernel(chunk, *refs),
            out_shape=jax.ShapeDtypeStruct((groups, height, LANES), BF16),
            compiler_params=WHOLE,
            name=f"pack{chunk}",
        )(*values)

    early = pack(0, rows + heads, x_in, dt_raw)
    late = pack(1, rows, x_in)
    early, late, bc_in = lax.optimization_barrier((early, late, bc_in))
    first = to_groups(early)
    gathered = lax.all_gather(bc_in, "head", axis=0, tiled=True)
    first, gathered, late = lax.optimization_barrier((first, gathered, late))
    second = to_groups(late)
    x_seg = [first[:, :rows].reshape(seg, LANES), second.reshape(seg, LANES)]
    dt_seg = first[:, rows:, :rows].transpose(1, 0, 2).reshape(heads, seg)
    par = jnp.stack([dt_bias, a_log])[:, :, None]
    par = jnp.broadcast_to(par, (2, heads, BLOCK))
    bc_rim = shift(gathered[seg - RIM :], "ctx", 1)
    c_mat, b_t, row_tab, col_tab = pl.pallas_call(
        prep_kernel,
        grid=(nblk,),
        in_specs=[
            rows_of(gathered.shape[1]),
            full((RIM, 2 * STATE)),
            full((4, 2 * STATE)),
            full((1, 2 * STATE)),
            lanes_of(heads),
            full(par.shape),
        ],
        out_specs=[rows_of(STATE), lanes_of(STATE), lanes_of(3 * heads), rows_of(2 * heads)],
        out_shape=[
            jax.ShapeDtypeStruct((seg, STATE), BF16),
            jax.ShapeDtypeStruct((STATE, seg), BF16),
            jax.ShapeDtypeStruct((3 * heads, seg), F32),
            jax.ShapeDtypeStruct((seg, 2 * heads), F32),
        ],
        scratch_shapes=[pltpu.VMEM((RIM, 2 * STATE), BF16)],
        compiler_params=PARAMS,
        name="prep",
    )(gathered, bc_rim, conv_bc, bias_bc[None, :], dt_seg, par)

    y_tok = []
    for j in range(CHUNKS):
        at = slice(LANES * j, LANES * (j + 1))
        rim = shift(x_seg[j][seg - RIM :], "ctx", 1)
        xc, local, summary = pl.pallas_call(
            lambda *refs, j=j: state_kernel(j, *refs),
            grid=(nblk,),
            in_specs=[
                rows_of(LANES),
                full((RIM, LANES)),
                full((4, LANES)),
                full((1, LANES)),
                lanes_of(STATE),
                lanes_of(3 * heads),
            ],
            out_specs=[
                rows_of(LANES),
                pl.BlockSpec((1, STATE + 8, LANES), lambda k: (k, 0, 0)),
                full((STATE + 8, LANES)),
            ],
            out_shape=[
                jax.ShapeDtypeStruct((seg, LANES), BF16),
                jax.ShapeDtypeStruct((nblk, STATE + 8, LANES), F32),
                jax.ShapeDtypeStruct((STATE + 8, LANES), F32),
            ],
            scratch_shapes=[pltpu.VMEM((RIM, LANES), BF16)],
            compiler_params=PARAMS,
            name=f"state{j}",
        )(x_seg[j], rim, conv_x[:, at], bias_x[None, at], b_t, row_tab)
        near, far = entering(summary)
        skip = jnp.repeat(d_skip[HEADS * j : HEADS * (j + 1)], WIDTH)[None, :]
        y_diag = pl.pallas_call(
            lambda *refs, j=j: diag_kernel(j, *refs),
            grid=(nblk,),
            in_specs=[
                rows_of(LANES),
                rows_of(STATE),
                lanes_of(STATE),
                lanes_of(3 * heads),
                rows_of(2 * heads),
                full((1, LANES)),
            ],
            out_specs=rows_of(LANES),
            out_shape=jax.ShapeDtypeStruct((seg, LANES), F32),
            compiler_params=PARAMS,
            name=f"diag{j}",
        )(xc, c_mat, b_t, row_tab, col_tab, skip)
        y = pl.pallas_call(
            lambda *refs, j=j: join_kernel(j, *refs),
            grid=(nblk,),
            in_specs=[
                rows_of(LANES),
                rows_of(STATE),
                rows_of(2 * heads),
                pl.BlockSpec((1, STATE + 8, LANES), lambda k: (k, 0, 0)),
                full((STATE + 8, LANES)),
                full((STATE + 8, LANES)),
            ],
            out_specs=rows_of(LANES),
            out_shape=jax.ShapeDtypeStruct((seg, LANES), BF16),
            compiler_params=PARAMS,
            name=f"join{j}",
        )(y_diag, c_mat, col_tab, local, near, far)
        y_tok.append(to_tokens(y))

    step = 32
    return pl.pallas_call(
        norm_kernel,
        grid=(rows // step,),
        in_specs=[
            pl.BlockSpec((groups, step, LANES), lambda k: (0, k, 0)),
            pl.BlockSpec((groups, step, LANES), lambda k: (0, k, 0)),
            pl.BlockSpec((step, z_in.shape[1]), lambda k: (k, 0)),
            full((1, z_in.shape[1])),
        ],
        out_specs=pl.BlockSpec((step, z_in.shape[1]), lambda k: (k, 0)),
        out_shape=jax.ShapeDtypeStruct(z_in.shape, BF16),
        scratch_shapes=[pltpu.VMEM((step, z_in.shape[1]), F32)],
        compiler_params=PARAMS,
        name="norm",
    )(y_tok[0], y_tok[1], z_in, norm_gain[None, :])


def solution(mesh):
    token = P(("ctx", "head"), None)
    in_specs = (
        token,
        token,
        token,
        token,
        P(None, "head"),
        P("head"),
        P(),
        P(),
        P("head"),
        P("head"),
        P("head"),
        P(),
    )
    return jax.shard_map(per_device, mesh=mesh, in_specs=in_specs, out_specs=token, check_vma=False)
```

```python
import jax
import jax.numpy as jnp
from jax import lax
from jax.experimental import pallas as pl
from jax.experimental.pallas import tpu as pltpu
from jax.sharding import PartitionSpec as P

BLOCK = 256
STATE = 128
WIDTH = 64
HEADS = 8
LANES = HEADS * WIDTH
PART = 256
RIM = 16
F32 = jnp.float32
BF16 = jnp.bfloat16


def silu(u):
    return u / (1.0 + jnp.exp(-u))


def causal_conv(before, rows, taps, offset):
    count = rows.shape[0]
    padded = jnp.concatenate([before, rows], 0).astype(F32)
    summed = offset + taps[0:1] * padded[RIM - 3 : RIM - 3 + count]
    summed = summed + taps[1:2] * padded[RIM - 2 : RIM - 2 + count]
    summed = summed + taps[2:3] * padded[RIM - 1 : RIM - 1 + count]
    summed = summed + taps[3:4] * padded[RIM : RIM + count]
    return silu(summed).astype(BF16)


def pack_kernel(x_ref, dt_ref, out_ref):
    rows = x_ref.shape[0]
    dt = dt_ref[...].astype(F32).T.astype(BF16)
    for g in range(out_ref.shape[0]):
        out_ref[g, :rows] = x_ref[:, LANES * g : LANES * (g + 1)]
        out_ref[g, rows:, :rows] = dt[HEADS * g : HEADS * (g + 1)]
        out_ref[g, rows:, rows:] = jnp.zeros((HEADS, LANES - rows), BF16)


def prep_kernel(g_ref, rim_ref, taps_ref, bias_ref, dt_ref, par_ref, c_ref, bt_ref, rows_ref, cols_ref, carry):
    @pl.when(pl.program_id(0) == 0)
    def _():
        carry[...] = rim_ref[...]

    raw = g_ref[...]
    bcc = causal_conv(carry[...], raw, taps_ref[...], bias_ref[...])
    carry[...] = raw[BLOCK - RIM :]
    c_ref[...] = bcc[:, STATE:]
    bt_ref[...] = bcc[:, :STATE].astype(F32).T.astype(BF16)
    shifted = dt_ref[...].astype(F32) + par_ref[0]
    dt = jnp.maximum(shifted, 0.0) + jnp.log1p(jnp.exp(-jnp.abs(shifted)))
    cs = dt * -jnp.exp(par_ref[1])
    lane = lax.broadcasted_iota(jnp.int32, cs.shape, 1)
    step = 1
    while step < BLOCK:
        cs = cs + jnp.where(lane >= step, pltpu.roll(cs, step, 1), 0.0)
        step *= 2
    tot = cs[:, BLOCK - 1 :]
    rows_ref[0:8] = cs
    rows_ref[8:16] = dt
    rows_ref[16:24] = jnp.exp(tot - cs) * dt
    cols_ref[...] = jnp.concatenate([cs, jnp.exp(cs)], 0).T


def lane_pair(first, second, shape):
    lane = lax.broadcasted_iota(jnp.int32, shape, 1)
    return jnp.where(lane < WIDTH, first, second)


def state_kernel(x_ref, rim_ref, taps_ref, bias_ref, bt_ref, rows_ref, xc_ref, local_ref, part_ref, carry, run):
    @pl.when(pl.program_id(0) == 0)
    def _():
        carry[...] = rim_ref[...]
        run[...] = jnp.zeros_like(run)

    raw = x_ref[...]
    xc = causal_conv(carry[...], raw, taps_ref[...], bias_ref[...])
    carry[...] = raw[BLOCK - RIM :]
    xc_ref[...] = xc
    local_ref[0] = run[...]
    bt = bt_ref[...].astype(F32)
    for pair in range(HEADS // 2):
        cols = slice(2 * WIDTH * pair, 2 * WIDTH * (pair + 1))
        parts, tots = [], []
        for h in (2 * pair, 2 * pair + 1):
            bw = (bt * rows_ref[16 + h : 17 + h]).astype(BF16)
            parts.append(jnp.dot(bw, xc[:, cols], preferred_element_type=F32))
            tots.append(rows_ref[h : h + 1, BLOCK - 1 :])
        tot = lane_pair(tots[0], tots[1], (1, 2 * WIDTH))
        st = lane_pair(parts[0], parts[1], (STATE, 2 * WIDTH))
        run[:STATE, cols] = run[:STATE, cols] * jnp.exp(tot) + st
        run[STATE:, cols] = run[STATE:, cols] + tot

    @pl.when(pl.program_id(0) == pl.num_programs(0) - 1)
    def _():
        part_ref[...] = jnp.zeros_like(part_ref)
        for i in range(STATE // 8):
            for j in range(LANES // PART):
                p = i * (LANES // PART) + j
                part_ref[p, :, :PART] = run[8 * i : 8 * (i + 1), PART * j : PART * (j + 1)]
                for half in range(PART // 128):
                    start = PART * j + 128 * half
                    part_ref[p, half : half + 1, PART:] = run[STATE : STATE + 1, start : start + 128]


def scan_kernel(part_ref, out_ref):
    run = jnp.zeros(out_ref.shape[1:], F32)
    for s in range(part_ref.shape[0]):
        out_ref[s] = run
        gain = jnp.concatenate([part_ref[s, half : half + 1, PART:] for half in range(PART // 128)], 1)
        run = run * jnp.exp(gain) + part_ref[s, :, :PART]


def diag_kernel(xc_ref, c_ref, bt_ref, rows_ref, cols_ref, skip_ref, y_ref):
    half = BLOCK // 2
    xc = xc_ref[...]
    scores = jnp.dot(c_ref[...], bt_ref[...], preferred_element_type=F32)
    for low, width in ((0, half), (half, BLOCK)):
        part = scores[low : low + half, :width]
        row = lax.broadcasted_iota(jnp.int32, (half, width), 0) + low
        col = lax.broadcasted_iota(jnp.int32, (half, width), 1)
        keep = row >= col
        for pair in range(HEADS // 2):
            cols = slice(2 * WIDTH * pair, 2 * WIDTH * (pair + 1))
            outs = []
            for h in (2 * pair, 2 * pair + 1):
                gap = cols_ref[low : low + half, h : h + 1] - rows_ref[h : h + 1, :width]
                spread = jnp.exp(jnp.where(keep, gap, -1e30))
                m = (part * spread * rows_ref[8 + h : 9 + h, :width]).astype(BF16)
                outs.append(jnp.dot(m, xc[:width, cols], preferred_element_type=F32))
            y = lane_pair(outs[0], outs[1], (half, 2 * WIDTH))
            y_ref[low : low + half, cols] = (
                y + skip_ref[:, cols] * xc[low : low + half, cols].astype(F32)
            )


def join_kernel(yd_ref, c_ref, cols_ref, local_ref, in_ref, y_ref, entry):
    @pl.when(pl.program_id(0) == 0)
    def _():
        for i in range(STATE // 8):
            for j in range(LANES // PART):
                piece = in_ref[i * (LANES // PART) + j]
                entry[8 * i : 8 * (i + 1), PART * j : PART * (j + 1)] = piece

    hb = (entry[...] * jnp.exp(local_ref[0, STATE : STATE + 1]) + local_ref[0, :STATE]).astype(BF16)
    off = jnp.dot(c_ref[...], hb, preferred_element_type=F32)
    for pair in range(HEADS // 2):
        cols = slice(2 * WIDTH * pair, 2 * WIDTH * (pair + 1))
        h = 8 + 2 * pair
        scale = lane_pair(cols_ref[:, h : h + 1], cols_ref[:, h + 1 : h + 2], (BLOCK, 2 * WIDTH))
        y_ref[:, cols] = (yd_ref[:, cols] + off[:, cols] * scale).astype(BF16)


def norm_kernel(y_ref, z_ref, gain_ref, out_ref, gated_ref):
    groups = y_ref.shape[0]
    total = jnp.zeros((z_ref.shape[0], 128), F32)
    for g in range(groups):
        at = slice(LANES * g, LANES * (g + 1))
        gated = y_ref[g].astype(F32) * silu(z_ref[:, at].astype(F32))
        gated_ref[:, at] = gated
        sq = gated * gated
        for start in range(0, LANES, 128):
            total = total + sq[:, start : start + 128]
    mean = jnp.sum(total, axis=1, keepdims=True) * (1.0 / (groups * LANES))
    out_ref[...] = (gated_ref[...] * lax.rsqrt(mean + 1e-05) * gain_ref[...]).astype(BF16)


def shift(value, axis, by):
    count = lax.axis_size(axis)
    return lax.ppermute(value, axis, [(i, i + by) for i in range(count - by)])


def entering(parts):
    count, height, _ = parts.shape
    got = lax.all_to_all(parts, "ctx", 0, 0, tiled=True)
    before = pl.pallas_call(
        scan_kernel,
        out_shape=jax.ShapeDtypeStruct((count, height, PART), F32),
        compiler_params=WHOLE,
        name="scan",
    )(got)
    return lax.all_to_all(before, "ctx", 0, 0, tiled=True)


def full(shape):
    return pl.BlockSpec(shape, lambda k: tuple(0 for _ in shape))


def rows_of(width):
    return pl.BlockSpec((BLOCK, width), lambda k: (k, 0))


def lanes_of(height):
    return pl.BlockSpec((height, BLOCK), lambda k: (0, k))


WHOLE = pltpu.CompilerParams(vmem_limit_bytes=16 << 20)
PARAMS = pltpu.CompilerParams(dimension_semantics=("arbitrary",), vmem_limit_bytes=16 << 20)


def per_device(
    x_in, dt_raw, bc_in, z_in, conv_x, bias_x, conv_bc, bias_bc, dt_bias, a_log, d_skip, norm_gain
):
    groups = lax.axis_size("head")
    rows = x_in.shape[0]
    seg = rows * groups
    nblk = seg // BLOCK
    heads = dt_bias.shape[0]

    def exchange(value):
        return lax.all_to_all(value.transpose(1, 0, 2), "head", 1, 1, tiled=True).transpose(1, 0, 2)

    packed = pl.pallas_call(
        pack_kernel,
        out_shape=jax.ShapeDtypeStruct((groups, rows + heads, LANES), BF16),
        compiler_params=WHOLE,
        name="pack",
    )(x_in, dt_raw)
    packed, bc_in = lax.optimization_barrier((packed, bc_in))
    first = exchange(packed)
    gathered = lax.all_gather(bc_in, "head", axis=0, tiled=True)
    x_seg = first[:, :rows].reshape(seg, LANES)
    dt_seg = first[:, rows:, :rows].transpose(1, 0, 2).reshape(heads, seg)
    par = jnp.stack([dt_bias, a_log])[:, :, None]
    par = jnp.broadcast_to(par, (2, heads, BLOCK))
    bc_rim = shift(gathered[seg - RIM :], "ctx", 1)
    c_mat, b_t, row_tab, col_tab = pl.pallas_call(
        prep_kernel,
        grid=(nblk,),
        in_specs=[
            rows_of(gathered.shape[1]),
            full((RIM, 2 * STATE)),
            full((4, 2 * STATE)),
            full((1, 2 * STATE)),
            lanes_of(heads),
            full(par.shape),
        ],
        out_specs=[rows_of(STATE), lanes_of(STATE), lanes_of(3 * heads), rows_of(2 * heads)],
        out_shape=[
            jax.ShapeDtypeStruct((seg, STATE), BF16),
            jax.ShapeDtypeStruct((STATE, seg), BF16),
            jax.ShapeDtypeStruct((3 * heads, seg), F32),
            jax.ShapeDtypeStruct((seg, 2 * heads), F32),
        ],
        scratch_shapes=[pltpu.VMEM((RIM, 2 * STATE), BF16)],
        compiler_params=PARAMS,
        name="prep",
    )(gathered, bc_rim, conv_bc, bias_bc[None, :], dt_seg, par)

    rim = shift(x_seg[seg - RIM :], "ctx", 1)
    pieces = (STATE // 8) * (LANES // PART)
    xc, local, parts = pl.pallas_call(
        state_kernel,
        grid=(nblk,),
        in_specs=[
            rows_of(LANES),
            full((RIM, LANES)),
            full((4, LANES)),
            full((1, LANES)),
            lanes_of(STATE),
            lanes_of(3 * heads),
        ],
        out_specs=[
            rows_of(LANES),
            pl.BlockSpec((1, STATE + 8, LANES), lambda k: (k, 0, 0)),
            full((pieces, 8, PART + 128)),
        ],
        out_shape=[
            jax.ShapeDtypeStruct((seg, LANES), BF16),
            jax.ShapeDtypeStruct((nblk, STATE + 8, LANES), F32),
            jax.ShapeDtypeStruct((pieces, 8, PART + 128), F32),
        ],
        scratch_shapes=[pltpu.VMEM((RIM, LANES), BF16), pltpu.VMEM((STATE + 8, LANES), F32)],
        compiler_params=PARAMS,
        name="state",
    )(x_seg, rim, conv_x, bias_x[None, :], b_t, row_tab)
    incoming = entering(parts)
    skip = jnp.repeat(d_skip, WIDTH)[None, :]
    y_diag = pl.pallas_call(
        diag_kernel,
        grid=(nblk,),
        in_specs=[
            rows_of(LANES),
            rows_of(STATE),
            lanes_of(STATE),
            lanes_of(3 * heads),
            rows_of(2 * heads),
            full((1, LANES)),
        ],
        out_specs=rows_of(LANES),
        out_shape=jax.ShapeDtypeStruct((seg, LANES), F32),
        compiler_params=PARAMS,
        name="diag",
    )(xc, c_mat, b_t, row_tab, col_tab, skip)
    y = pl.pallas_call(
        join_kernel,
        grid=(nblk,),
        in_specs=[
            rows_of(LANES),
            rows_of(STATE),
            rows_of(2 * heads),
            pl.BlockSpec((1, STATE + 8, LANES), lambda k: (k, 0, 0)),
            full((pieces, 8, PART)),
        ],
        out_specs=rows_of(LANES),
        out_shape=jax.ShapeDtypeStruct((seg, LANES), BF16),
        scratch_shapes=[pltpu.VMEM((STATE, LANES), F32)],
        compiler_params=PARAMS,
        name="join",
    )(y_diag, c_mat, col_tab, local, incoming)
    y_tok = exchange(y.reshape(groups, rows, LANES))
    step = 32
    return pl.pallas_call(
        norm_kernel,
        grid=(rows // step,),
        in_specs=[
            pl.BlockSpec((groups, step, LANES), lambda k: (0, k, 0)),
            pl.BlockSpec((step, z_in.shape[1]), lambda k: (k, 0)),
            full((1, z_in.shape[1])),
        ],
        out_specs=pl.BlockSpec((step, z_in.shape[1]), lambda k: (k, 0)),
        out_shape=jax.ShapeDtypeStruct(z_in.shape, BF16),
        scratch_shapes=[pltpu.VMEM((step, z_in.shape[1]), F32)],
        compiler_params=PARAMS,
        name="norm",
    )(y_tok, z_in, norm_gain[None, :])


def solution(mesh):
    token = P(("ctx", "head"), None)
    in_specs = (
        token,
        token,
        token,
        token,
        P(None, "head"),
        P("head"),
        P(),
        P(),
        P("head"),
        P("head"),
        P("head"),
        P(),
    )
    return jax.shard_map(per_device, mesh=mesh, in_specs=in_specs, out_specs=token, check_vma=False)
```

```python
import jax
import jax.numpy as jnp
from jax import lax
from jax.experimental import pallas as pl
from jax.experimental.pallas import tpu as pltpu
from jax.sharding import PartitionSpec as P

BLOCK = 256
STATE = 128
WIDTH = 64
HEADS = 8
LANES = HEADS * WIDTH
PART = 256
RIM = 8
F32 = jnp.float32
BF16 = jnp.bfloat16


def silu(u):
    return u / (1.0 + jnp.exp(-u))


def causal_conv(before, rows, taps, offset):
    count = rows.shape[0]
    padded = jnp.concatenate([before, rows.astype(F32)], 0)
    summed = offset + taps[0:1] * padded[RIM - 3 : RIM - 3 + count]
    summed = summed + taps[1:2] * padded[RIM - 2 : RIM - 2 + count]
    summed = summed + taps[2:3] * padded[RIM - 1 : RIM - 1 + count]
    summed = summed + taps[3:4] * padded[RIM : RIM + count]
    return silu(summed).astype(BF16)


def pack_kernel(x_ref, dt_ref, tail_ref, out_ref):
    rows = x_ref.shape[0]
    dt = dt_ref[...].astype(F32).T
    wide = LANES - 128
    row = lax.broadcasted_iota(jnp.int32, (RIM, wide), 0)
    for g in range(out_ref.shape[0]):
        start = LANES * g
        out_ref[g, :rows] = x_ref[:, start : start + LANES]
        tail = tail_ref[:, start : start + LANES].astype(F32)
        rest = jnp.concatenate([tail[:, wide:], jnp.zeros((RIM, wide - 128), F32)], 1)
        spare = jnp.where(row < 6, pltpu.roll(rest, 6, 0), 0.0)
        spare = jnp.where(row < 3, pltpu.roll(tail[:, :wide], 3, 0), spare)
        head = jnp.concatenate([dt[HEADS * g : HEADS * (g + 1)], jnp.zeros((HEADS, 128 - rows), F32)], 1)
        out_ref[g, rows:] = jnp.concatenate([head, spare], 1).astype(BF16)


def prep_kernel(g_ref, rim_ref, taps_ref, bias_ref, c_ref, bt_ref, carry):
    @pl.when(pl.program_id(0) == 0)
    def _():
        carry[...] = rim_ref[...].astype(F32)

    raw = g_ref[...]
    bcc = causal_conv(carry[...], raw, taps_ref[...], bias_ref[...])
    carry[...] = raw[BLOCK - RIM :].astype(F32)
    c_ref[...] = bcc[:, STATE:]
    bt_ref[...] = bcc[:, :STATE].astype(F32).T.astype(BF16)


def step_tables(dt_raw, par):
    shifted = dt_raw.astype(F32) + par[0]
    dt = jnp.maximum(shifted, 0.0) + jnp.log1p(jnp.exp(-jnp.abs(shifted)))
    cs = dt * -jnp.exp(par[1])
    lane = lax.broadcasted_iota(jnp.int32, cs.shape, 1)
    step = 1
    while step < BLOCK:
        cs = cs + jnp.where(lane >= step, pltpu.roll(cs, step, 1), 0.0)
        step *= 2
    return cs, dt


def lane_pair(first, second, shape):
    lane = lax.broadcasted_iota(jnp.int32, shape, 1)
    return jnp.where(lane < WIDTH, first, second)


def state_kernel(
    x_ref, spare_ref, taps_ref, bias_ref, bt_ref, dt_ref, par_ref,
    xc_ref, local_ref, part_ref, rows_ref, cols_ref, carry, run
):
    @pl.when(pl.program_id(0) == 0)
    def _():
        spare = spare_ref[...].astype(F32)
        most = pltpu.roll(spare[:, 128:], 5, 0)
        rest = pltpu.roll(spare[:, 128:256], 2, 0)
        carry[...] = jnp.concatenate([most, rest], 1)
        run[...] = jnp.zeros_like(run)

    cs, dt = step_tables(dt_ref[...], par_ref)
    weight = jnp.exp(cs[:, BLOCK - 1 :] - cs) * dt
    rows_ref[:HEADS] = cs
    rows_ref[HEADS:] = dt
    cols_ref[...] = jnp.concatenate([cs, jnp.exp(cs)], 0).T
    raw = x_ref[...]
    xc = causal_conv(carry[...], raw, taps_ref[...], bias_ref[...])
    carry[...] = raw[BLOCK - RIM :].astype(F32)
    xc_ref[...] = xc
    local_ref[0] = run[...]
    bt = bt_ref[...].astype(F32)
    for pair in range(HEADS // 2):
        cols = slice(2 * WIDTH * pair, 2 * WIDTH * (pair + 1))
        parts, tots = [], []
        for h in (2 * pair, 2 * pair + 1):
            bw = (bt * weight[h : h + 1]).astype(BF16)
            parts.append(jnp.dot(bw, xc[:, cols], preferred_element_type=F32))
            tots.append(cs[h : h + 1, BLOCK - 1 :])
        tot = lane_pair(tots[0], tots[1], (1, 2 * WIDTH))
        st = lane_pair(parts[0], parts[1], (STATE, 2 * WIDTH))
        run[:STATE, cols] = run[:STATE, cols] * jnp.exp(tot) + st
        run[STATE:, cols] = run[STATE:, cols] + tot

    @pl.when(pl.program_id(0) == pl.num_programs(0) - 1)
    def _():
        part_ref[...] = jnp.zeros_like(part_ref)
        for i in range(STATE // 8):
            for j in range(LANES // PART):
                p = i * (LANES // PART) + j
                part_ref[p, :, :PART] = run[8 * i : 8 * (i + 1), PART * j : PART * (j + 1)]
                for half in range(PART // 128):
                    start = PART * j + 128 * half
                    part_ref[p, half : half + 1, PART:] = run[STATE : STATE + 1, start : start + 128]


def scan_kernel(part_ref, out_ref):
    run = jnp.zeros(out_ref.shape[1:], F32)
    for s in range(part_ref.shape[0]):
        out_ref[s] = run
        gain = jnp.concatenate([part_ref[s, half : half + 1, PART:] for half in range(PART // 128)], 1)
        run = run * jnp.exp(gain) + part_ref[s, :, :PART]


def diag_kernel(xc_ref, c_ref, bt_ref, rows_ref, cols_ref, skip_ref, y_ref):
    half = BLOCK // 2
    xc = xc_ref[...]
    scores = jnp.dot(c_ref[...], bt_ref[...], preferred_element_type=F32)
    for low, width in ((0, half), (half, BLOCK)):
        part = scores[low : low + half, :width]
        row = lax.broadcasted_iota(jnp.int32, (half, width), 0) + low
        col = lax.broadcasted_iota(jnp.int32, (half, width), 1)
        keep = row >= col
        for pair in range(HEADS // 2):
            cols = slice(2 * WIDTH * pair, 2 * WIDTH * (pair + 1))
            outs = []
            for h in (2 * pair, 2 * pair + 1):
                gap = cols_ref[low : low + half, h : h + 1] - rows_ref[h : h + 1, :width]
                spread = jnp.exp(jnp.where(keep, gap, -1e30))
                m = (part * spread * rows_ref[8 + h : 9 + h, :width]).astype(BF16)
                outs.append(jnp.dot(m, xc[:width, cols], preferred_element_type=F32))
            y = lane_pair(outs[0], outs[1], (half, 2 * WIDTH))
            y_ref[low : low + half, cols] = (
                y + skip_ref[:, cols] * xc[low : low + half, cols].astype(F32)
            )


def join_kernel(yd_ref, c_ref, cols_ref, local_ref, in_ref, y_ref, entry):
    @pl.when(pl.program_id(0) == 0)
    def _():
        for i in range(STATE // 8):
            for j in range(LANES // PART):
                piece = in_ref[i * (LANES // PART) + j]
                entry[8 * i : 8 * (i + 1), PART * j : PART * (j + 1)] = piece

    hb = (entry[...] * jnp.exp(local_ref[0, STATE : STATE + 1]) + local_ref[0, :STATE]).astype(BF16)
    off = jnp.dot(c_ref[...], hb, preferred_element_type=F32)
    for pair in range(HEADS // 2):
        cols = slice(2 * WIDTH * pair, 2 * WIDTH * (pair + 1))
        h = 8 + 2 * pair
        scale = lane_pair(cols_ref[:, h : h + 1], cols_ref[:, h + 1 : h + 2], (BLOCK, 2 * WIDTH))
        y_ref[:, cols] = (yd_ref[:, cols] + off[:, cols] * scale).astype(BF16)


def gate_kernel(z_ref, out_ref):
    out_ref[...] = silu(z_ref[...].astype(F32))


def norm_kernel(y_ref, gate_ref, gain_ref, out_ref, gated_ref):
    groups = y_ref.shape[0]
    total = jnp.zeros((gate_ref.shape[0], 128), F32)
    for g in range(groups):
        at = slice(LANES * g, LANES * (g + 1))
        gated = y_ref[g].astype(F32) * gate_ref[:, at]
        gated_ref[:, at] = gated
        sq = gated * gated
        for start in range(0, LANES, 128):
            total = total + sq[:, start : start + 128]
    mean = jnp.sum(total, axis=1, keepdims=True) * (1.0 / (groups * LANES))
    out_ref[...] = (gated_ref[...] * lax.rsqrt(mean + 1e-05) * gain_ref[...]).astype(BF16)


def shift(value, axis, by):
    count = lax.axis_size(axis)
    return lax.ppermute(value, axis, [(i, i + by) for i in range(count - by)])


def entering(parts):
    count, height, _ = parts.shape
    got = lax.all_to_all(parts, "ctx", 0, 0, tiled=True)
    before = pl.pallas_call(
        scan_kernel,
        out_shape=jax.ShapeDtypeStruct((count, height, PART), F32),
        compiler_params=WHOLE,
        name="scan",
    )(got)
    return lax.all_to_all(before, "ctx", 0, 0, tiled=True)


def held(value):
    return pltpu.with_memory_space_constraint(value, pltpu.HBM)


def full(shape):
    return pl.BlockSpec(shape, lambda k: tuple(0 for _ in shape))


def rows_of(width):
    return pl.BlockSpec((BLOCK, width), lambda k: (k, 0))


def lanes_of(height):
    return pl.BlockSpec((height, BLOCK), lambda k: (0, k))


WHOLE = pltpu.CompilerParams(vmem_limit_bytes=16 << 20)
PARAMS = pltpu.CompilerParams(dimension_semantics=("arbitrary",), vmem_limit_bytes=16 << 20)


def per_device(
    x_in, dt_raw, bc_in, z_in, conv_x, bias_x, conv_bc, bias_bc, dt_bias, a_log, d_skip, norm_gain
):
    groups = lax.axis_size("head")
    rows = x_in.shape[0]
    seg = rows * groups
    nblk = seg // BLOCK
    heads = dt_bias.shape[0]

    def exchange(value):
        return lax.all_to_all(value.transpose(1, 0, 2), "head", 1, 1, tiled=True).transpose(1, 0, 2)

    tail = shift(x_in[rows - RIM :], "ctx", 1)
    gathered = lax.all_gather(bc_in, "head", axis=0, tiled=True)
    tail, gathered = lax.optimization_barrier((tail, gathered))
    packed = pl.pallas_call(
        pack_kernel,
        out_shape=jax.ShapeDtypeStruct((groups, rows + RIM, LANES), BF16),
        compiler_params=WHOLE,
        name="pack",
    )(x_in, dt_raw, tail)
    first = exchange(packed)
    x_seg = first[:, :rows].reshape(seg, LANES)
    dt_seg = first[:, rows:, :rows].transpose(1, 0, 2).reshape(heads, seg)
    par = jnp.stack([dt_bias, a_log])[:, :, None]
    par = jnp.broadcast_to(par, (2, heads, BLOCK))
    bc_rim = shift(gathered[seg - RIM :], "ctx", 1)
    c_mat, b_t = pl.pallas_call(
        prep_kernel,
        grid=(nblk,),
        in_specs=[
            rows_of(2 * STATE),
            full((RIM, 2 * STATE)),
            full((4, 2 * STATE)),
            full((1, 2 * STATE)),
        ],
        out_specs=[rows_of(STATE), lanes_of(STATE)],
        out_shape=[pltpu.HBM((seg, STATE), BF16), pltpu.HBM((STATE, seg), BF16)],
        scratch_shapes=[pltpu.VMEM((RIM, 2 * STATE), F32)],
        compiler_params=PARAMS,
        name="prep",
    )(gathered, bc_rim, conv_bc, bias_bc[None, :])
    pieces = (STATE // 8) * (LANES // PART)
    xc, local, parts, row_tab, col_tab = pl.pallas_call(
        state_kernel,
        grid=(nblk,),
        in_specs=[
            rows_of(LANES),
            full((RIM, LANES)),
            full((4, LANES)),
            full((1, LANES)),
            lanes_of(STATE),
            lanes_of(heads),
            full(par.shape),
        ],
        out_specs=[
            rows_of(LANES),
            pl.BlockSpec((1, STATE + 8, LANES), lambda k: (k, 0, 0)),
            full((pieces, 8, PART + 128)),
            lanes_of(2 * heads),
            rows_of(2 * heads),
        ],
        out_shape=[
            pltpu.HBM((seg, LANES), BF16),
            pltpu.HBM((nblk, STATE + 8, LANES), F32),
            jax.ShapeDtypeStruct((pieces, 8, PART + 128), F32),
            pltpu.HBM((2 * heads, seg), F32),
            pltpu.HBM((seg, 2 * heads), F32),
        ],
        scratch_shapes=[pltpu.VMEM((RIM, LANES), F32), pltpu.VMEM((STATE + 8, LANES), F32)],
        compiler_params=PARAMS,
        name="state",
    )(x_seg, first[groups - 1, rows:], conv_x, bias_x[None, :], held(b_t), dt_seg, par)
    c_mat, b_t, xc, local, row_tab, col_tab = [held(v) for v in (c_mat, b_t, xc, local, row_tab, col_tab)]
    incoming = entering(parts)
    skip = jnp.repeat(d_skip, WIDTH)[None, :]
    y_diag = pl.pallas_call(
        diag_kernel,
        grid=(nblk,),
        in_specs=[
            rows_of(LANES),
            rows_of(STATE),
            lanes_of(STATE),
            lanes_of(2 * heads),
            rows_of(2 * heads),
            full((1, LANES)),
        ],
        out_specs=rows_of(LANES),
        out_shape=pltpu.HBM((seg, LANES), F32),
        compiler_params=PARAMS,
        name="diag",
    )(xc, c_mat, b_t, row_tab, col_tab, skip)
    y = pl.pallas_call(
        join_kernel,
        grid=(nblk,),
        in_specs=[
            rows_of(LANES),
            rows_of(STATE),
            rows_of(2 * heads),
            pl.BlockSpec((1, STATE + 8, LANES), lambda k: (k, 0, 0)),
            full((pieces, 8, PART)),
        ],
        out_specs=rows_of(LANES),
        out_shape=jax.ShapeDtypeStruct((seg, LANES), BF16),
        scratch_shapes=[pltpu.VMEM((STATE, LANES), F32)],
        compiler_params=PARAMS,
        name="join",
    )(held(y_diag), c_mat, col_tab, local, incoming)
    y_tok = exchange(y.reshape(groups, rows, LANES))
    step = 32
    gate = pl.pallas_call(
        gate_kernel,
        grid=(rows // step,),
        in_specs=[pl.BlockSpec((step, z_in.shape[1]), lambda k: (k, 0))],
        out_specs=pl.BlockSpec((step, z_in.shape[1]), lambda k: (k, 0)),
        out_shape=jax.ShapeDtypeStruct(z_in.shape, F32),
        compiler_params=PARAMS,
        name="gate",
    )(z_in)
    return pl.pallas_call(
        norm_kernel,
        grid=(rows // step,),
        in_specs=[
            pl.BlockSpec((groups, step, LANES), lambda k: (0, k, 0)),
            pl.BlockSpec((step, z_in.shape[1]), lambda k: (k, 0)),
            full((1, z_in.shape[1])),
        ],
        out_specs=pl.BlockSpec((step, z_in.shape[1]), lambda k: (k, 0)),
        out_shape=jax.ShapeDtypeStruct(z_in.shape, BF16),
        scratch_shapes=[pltpu.VMEM((step, z_in.shape[1]), F32)],
        compiler_params=PARAMS,
        name="norm",
    )(y_tok, gate, norm_gain[None, :])


def solution(mesh):
    token = P(("ctx", "head"), None)
    in_specs = (
        token,
        token,
        token,
        token,
        P(None, "head"),
        P("head"),
        P(),
        P(),
        P("head"),
        P("head"),
        P("head"),
        P(),
    )
    return jax.shard_map(per_device, mesh=mesh, in_specs=in_specs, out_specs=token, check_vma=False)
```

```python
import jax
import jax.numpy as jnp
from jax import lax
from jax.experimental import pallas as pl
from jax.experimental.pallas import tpu as pltpu
from jax.sharding import PartitionSpec as P

BLOCK = 256
STATE = 128
WIDTH = 64
HEADS = 8
LANES = HEADS * WIDTH
PART = 256
RIM = 8
F32 = jnp.float32
BF16 = jnp.bfloat16


def silu(u):
    return u / (1.0 + jnp.exp(-u))


def causal_conv(before, rows, taps, offset):
    count = rows.shape[0]
    padded = jnp.concatenate([before, rows.astype(F32)], 0)
    summed = offset + taps[0:1] * padded[RIM - 3 : RIM - 3 + count]
    summed = summed + taps[1:2] * padded[RIM - 2 : RIM - 2 + count]
    summed = summed + taps[2:3] * padded[RIM - 1 : RIM - 1 + count]
    summed = summed + taps[3:4] * padded[RIM : RIM + count]
    return silu(summed).astype(BF16)


def pack_kernel(x_ref, dt_ref, tail_ref, out_ref, dt_t):
    rows = x_ref.shape[0]
    count = out_ref.shape[0]

    @pl.when(pl.program_id(0) == 0)
    def _():
        dt_t[...] = dt_ref[...].astype(F32).T

    wide = LANES - 128
    row = lax.broadcasted_iota(jnp.int32, (RIM, wide), 0)
    for g in range(count):
        start = LANES * g
        out_ref[g, :rows] = x_ref[:, start : start + LANES]
        tail = tail_ref[:, start : start + LANES].astype(F32)
        rest = jnp.concatenate([tail[:, wide:], jnp.zeros((RIM, wide - 128), F32)], 1)
        spare = jnp.where(row < 6, pltpu.roll(rest, 6, 0), 0.0)
        spare = jnp.where(row < 3, pltpu.roll(tail[:, :wide], 3, 0), spare)
        first = pl.multiple_of(HEADS * (count * pl.program_id(0) + g), HEADS)
        head = jnp.concatenate([dt_t[pl.ds(first, HEADS)], jnp.zeros((HEADS, 128 - rows), F32)], 1)
        out_ref[g, rows:] = jnp.concatenate([head, spare], 1).astype(BF16)


def prep_kernel(g_ref, rim_ref, taps_ref, bias_ref, c_ref, bt_ref, carry):
    @pl.when(pl.program_id(0) == 0)
    def _():
        carry[...] = rim_ref[...].astype(F32)

    raw = g_ref[...]
    bcc = causal_conv(carry[...], raw, taps_ref[...], bias_ref[...])
    carry[...] = raw[BLOCK - RIM :].astype(F32)
    c_ref[...] = bcc[:, STATE:]
    bt_ref[...] = bcc[:, :STATE].astype(F32).T.astype(BF16)


def step_tables(dt_raw, par):
    shifted = dt_raw.astype(F32) + par[0]
    dt = jnp.maximum(shifted, 0.0) + jnp.log1p(jnp.exp(-jnp.abs(shifted)))
    cs = dt * -jnp.exp(par[1])
    lane = lax.broadcasted_iota(jnp.int32, cs.shape, 1) & (BLOCK - 1)
    step = 1
    while step < BLOCK:
        cs = cs + jnp.where(lane >= step, pltpu.roll(cs, step, 1), 0.0)
        step *= 2
    return cs, dt


def lane_pair(first, second, shape):
    lane = lax.broadcasted_iota(jnp.int32, shape, 1)
    return jnp.where(lane < WIDTH, first, second)


def state_kernel(
    x_ref, spare_ref, taps_ref, bias_ref, bt_ref, dt_ref, par_ref,
    xc_ref, local_ref, part_ref, rows_ref, carry, run
):
    @pl.when(pl.program_id(0) == 0)
    def _():
        spare = spare_ref[...].astype(F32)
        most = pltpu.roll(spare[:, 128:], 5, 0)
        rest = pltpu.roll(spare[:, 128:256], 2, 0)
        carry[...] = jnp.concatenate([most, rest], 1)
        run[...] = jnp.zeros_like(run)
        rows_ref[:HEADS], rows_ref[HEADS:] = step_tables(dt_ref[...], par_ref)

    here = pl.ds(pl.multiple_of(BLOCK * pl.program_id(0), BLOCK), BLOCK)
    cs = rows_ref[:HEADS, here]
    weight = jnp.exp(cs[:, BLOCK - 1 :] - cs) * rows_ref[HEADS:, here]
    raw = x_ref[...]
    xc = causal_conv(carry[...], raw, taps_ref[...], bias_ref[...])
    carry[...] = raw[BLOCK - RIM :].astype(F32)
    xc_ref[...] = xc
    local_ref[0] = run[...]
    bt = bt_ref[...].astype(F32)
    for pair in range(HEADS // 2):
        cols = slice(2 * WIDTH * pair, 2 * WIDTH * (pair + 1))
        parts, tots = [], []
        for h in (2 * pair, 2 * pair + 1):
            bw = (bt * weight[h : h + 1]).astype(BF16)
            parts.append(jnp.dot(bw, xc[:, cols], preferred_element_type=F32))
            tots.append(cs[h : h + 1, BLOCK - 1 :])
        tot = lane_pair(tots[0], tots[1], (1, 2 * WIDTH))
        st = lane_pair(parts[0], parts[1], (STATE, 2 * WIDTH))
        run[:STATE, cols] = run[:STATE, cols] * jnp.exp(tot) + st
        run[STATE:, cols] = run[STATE:, cols] + tot

    @pl.when(pl.program_id(0) == pl.num_programs(0) - 1)
    def _():
        part_ref[...] = jnp.zeros_like(part_ref)
        for i in range(STATE // 8):
            for j in range(LANES // PART):
                p = i * (LANES // PART) + j
                part_ref[p, :, :PART] = run[8 * i : 8 * (i + 1), PART * j : PART * (j + 1)]
                for half in range(PART // 128):
                    start = PART * j + 128 * half
                    part_ref[p, half : half + 1, PART:] = run[STATE : STATE + 1, start : start + 128]


def scan_kernel(part_ref, out_ref):
    run = jnp.zeros(out_ref.shape[1:], F32)
    for s in range(part_ref.shape[0]):
        out_ref[s] = run
        gain = jnp.concatenate([part_ref[s, half : half + 1, PART:] for half in range(PART // 128)], 1)
        run = run * jnp.exp(gain) + part_ref[s, :, :PART]


def diag_kernel(xc_ref, c_ref, bt_ref, rows_ref, skip_ref, y_ref):
    cs_t = rows_ref[:HEADS].T
    half = BLOCK // 2
    xc = xc_ref[...]
    scores = jnp.dot(c_ref[...], bt_ref[...], preferred_element_type=F32)
    for low, width in ((0, half), (half, BLOCK)):
        part = scores[low : low + half, :width]
        row = lax.broadcasted_iota(jnp.int32, (half, width), 0) + low
        col = lax.broadcasted_iota(jnp.int32, (half, width), 1)
        keep = row >= col
        for pair in range(HEADS // 2):
            cols = slice(2 * WIDTH * pair, 2 * WIDTH * (pair + 1))
            outs = []
            for h in (2 * pair, 2 * pair + 1):
                gap = cs_t[low : low + half, h : h + 1] - rows_ref[h : h + 1, :width]
                spread = jnp.exp(jnp.where(keep, gap, -1e30))
                m = (part * spread * rows_ref[8 + h : 9 + h, :width]).astype(BF16)
                outs.append(jnp.dot(m, xc[:width, cols], preferred_element_type=F32))
            y = lane_pair(outs[0], outs[1], (half, 2 * WIDTH))
            y_ref[low : low + half, cols] = (
                y + skip_ref[:, cols] * xc[low : low + half, cols].astype(F32)
            )


def join_kernel(upper_ref, lower_ref, c_ref, rows_ref, local_ref, in_ref, y_ref, entry):
    @pl.when(pl.program_id(0) == 0)
    def _():
        for i in range(STATE // 8):
            for j in range(LANES // PART):
                piece = in_ref[i * (LANES // PART) + j]
                entry[8 * i : 8 * (i + 1), PART * j : PART * (j + 1)] = piece

    hb = (entry[...] * jnp.exp(local_ref[0, STATE : STATE + 1]) + local_ref[0, :STATE]).astype(BF16)
    off = jnp.dot(c_ref[...], hb, preferred_element_type=F32)
    grow = jnp.exp(rows_ref[:HEADS]).T

    def finish(diag_ref):
        for pair in range(HEADS // 2):
            cols = slice(2 * WIDTH * pair, 2 * WIDTH * (pair + 1))
            h = 2 * pair
            scale = lane_pair(grow[:, h : h + 1], grow[:, h + 1 : h + 2], (BLOCK, 2 * WIDTH))
            y_ref[:, cols] = (diag_ref[:, cols] + off[:, cols] * scale).astype(BF16)

    early = pl.program_id(0) < pl.num_programs(0) // 2
    pl.when(early)(lambda: finish(upper_ref))
    pl.when(jnp.logical_not(early))(lambda: finish(lower_ref))


def gate_kernel(z_ref, out_ref):
    out_ref[...] = silu(z_ref[...].astype(F32))


def norm_kernel(y_ref, gate_ref, gain_ref, out_ref, gated_ref):
    groups = y_ref.shape[0]
    total = jnp.zeros((gate_ref.shape[0], 128), F32)
    for g in range(groups):
        at = slice(LANES * g, LANES * (g + 1))
        gated = y_ref[g].astype(F32) * gate_ref[:, at]
        gated_ref[:, at] = gated
        sq = gated * gated
        for start in range(0, LANES, 128):
            total = total + sq[:, start : start + 128]
    mean = jnp.sum(total, axis=1, keepdims=True) * (1.0 / (groups * LANES))
    out_ref[...] = (gated_ref[...] * lax.rsqrt(mean + 1e-05) * gain_ref[...]).astype(BF16)


def shift(value, axis, by):
    count = lax.axis_size(axis)
    return lax.ppermute(value, axis, [(i, i + by) for i in range(count - by)])


def held(value):
    return pltpu.with_memory_space_constraint(value, pltpu.HBM)


def full(shape):
    return pl.BlockSpec(shape, lambda k: tuple(0 for _ in shape))


def rows_of(width, first=0):
    return pl.BlockSpec((BLOCK, width), lambda k: (k + first, 0))


def lanes_of(height, first=0):
    return pl.BlockSpec((height, BLOCK), lambda k: (0, k + first))


WHOLE = pltpu.CompilerParams(vmem_limit_bytes=16 << 20)
PARAMS = pltpu.CompilerParams(dimension_semantics=("arbitrary",), vmem_limit_bytes=16 << 20)


def per_device(
    x_in, dt_raw, bc_in, z_in, conv_x, bias_x, conv_bc, bias_bc, dt_bias, a_log, d_skip, norm_gain
):
    groups = lax.axis_size("head")
    rows = x_in.shape[0]
    seg = rows * groups
    nblk = seg // BLOCK
    heads = dt_bias.shape[0]

    def exchange(value):
        return lax.all_to_all(value.transpose(1, 0, 2), "head", 1, 1, tiled=True).transpose(1, 0, 2)

    tail = shift(x_in[rows - RIM :], "ctx", 1)
    gathered = lax.all_gather(bc_in, "head", axis=0, tiled=True)
    tail, gathered = lax.optimization_barrier((tail, gathered))
    steps = 4
    packed = pl.pallas_call(
        pack_kernel,
        grid=(steps,),
        in_specs=[
            pl.BlockSpec((rows, x_in.shape[1] // steps), lambda k: (0, k)),
            full(dt_raw.shape),
            pl.BlockSpec((RIM, x_in.shape[1] // steps), lambda k: (0, k)),
        ],
        out_specs=pl.BlockSpec((groups // steps, rows + RIM, LANES), lambda k: (k, 0, 0)),
        out_shape=jax.ShapeDtypeStruct((groups, rows + RIM, LANES), BF16),
        scratch_shapes=[pltpu.VMEM((dt_raw.shape[1], rows), F32)],
        compiler_params=PARAMS,
        name="pack",
    )(held(x_in), dt_raw, tail)
    first = exchange(packed)
    x_seg = first[:, :rows].reshape(seg, LANES)
    dt_seg = first[:, rows:, :rows].transpose(1, 0, 2).reshape(heads, seg)
    par = jnp.stack([dt_bias, a_log])[:, :, None]
    par = jnp.broadcast_to(par, (2, heads, seg))
    bc_rim = shift(gathered[seg - RIM :], "ctx", 1)
    c_mat, b_t = pl.pallas_call(
        prep_kernel,
        grid=(nblk,),
        in_specs=[
            rows_of(2 * STATE),
            full((RIM, 2 * STATE)),
            full((4, 2 * STATE)),
            full((1, 2 * STATE)),
        ],
        out_specs=[rows_of(STATE), lanes_of(STATE)],
        out_shape=[pltpu.HBM((seg, STATE), BF16), pltpu.HBM((STATE, seg), BF16)],
        scratch_shapes=[pltpu.VMEM((RIM, 2 * STATE), F32)],
        compiler_params=PARAMS,
        name="prep",
    )(gathered, bc_rim, conv_bc, bias_bc[None, :])
    pieces = (STATE // 8) * (LANES // PART)
    xc, local, parts, row_tab = pl.pallas_call(
        state_kernel,
        grid=(nblk,),
        in_specs=[
            rows_of(LANES),
            full((RIM, LANES)),
            full((4, LANES)),
            full((1, LANES)),
            lanes_of(STATE),
            full(dt_seg.shape),
            full(par.shape),
        ],
        out_specs=[
            rows_of(LANES),
            pl.BlockSpec((1, STATE + 8, LANES), lambda k: (k, 0, 0)),
            full((pieces, 8, PART + 128)),
            full((2 * heads, seg)),
        ],
        out_shape=[
            pltpu.HBM((seg, LANES), BF16),
            pltpu.HBM((nblk, STATE + 8, LANES), F32),
            jax.ShapeDtypeStruct((pieces, 8, PART + 128), F32),
            pltpu.HBM((2 * heads, seg), F32),
        ],
        scratch_shapes=[pltpu.VMEM((RIM, LANES), F32), pltpu.VMEM((STATE + 8, LANES), F32)],
        compiler_params=PARAMS,
        name="state",
    )(x_seg, first[groups - 1, rows:], conv_x, bias_x[None, :], held(b_t), dt_seg, par)
    c_mat, b_t, local, row_tab = [held(v) for v in (c_mat, b_t, local, row_tab)]
    skip = jnp.repeat(d_skip, WIDTH)[None, :]
    half = nblk // 2

    def diagonal(first_block):
        return pl.pallas_call(
            diag_kernel,
            grid=(half,),
            in_specs=[
                rows_of(LANES, first_block),
                rows_of(STATE, first_block),
                lanes_of(STATE, first_block),
                lanes_of(2 * heads, first_block),
                full((1, LANES)),
            ],
            out_specs=rows_of(LANES),
            out_shape=pltpu.HBM((half * BLOCK, LANES), F32),
            compiler_params=PARAMS,
            name="diag",
        )(held(xc), c_mat, b_t, row_tab, skip)

    upper = diagonal(0)
    got = lax.all_to_all(parts, "ctx", 0, 0, tiled=True)
    got, xc, upper = lax.optimization_barrier((got, xc, upper))
    before = pl.pallas_call(
        scan_kernel,
        out_shape=jax.ShapeDtypeStruct((pieces, 8, PART), F32),
        compiler_params=WHOLE,
        name="scan",
    )(got)
    incoming = lax.all_to_all(before, "ctx", 0, 0, tiled=True)
    lower = diagonal(half)
    y = pl.pallas_call(
        join_kernel,
        grid=(nblk,),
        in_specs=[
            pl.BlockSpec((BLOCK, LANES), lambda k: (jnp.minimum(k, half - 1), 0)),
            pl.BlockSpec((BLOCK, LANES), lambda k: (jnp.maximum(k - half, 0), 0)),
            rows_of(STATE),
            lanes_of(2 * heads),
            pl.BlockSpec((1, STATE + 8, LANES), lambda k: (k, 0, 0)),
            full((pieces, 8, PART)),
        ],
        out_specs=rows_of(LANES),
        out_shape=pltpu.HBM((seg, LANES), BF16),
        scratch_shapes=[pltpu.VMEM((STATE, LANES), F32)],
        compiler_params=PARAMS,
        name="join",
    )(held(upper), held(lower), c_mat, row_tab, local, incoming)
    y_tok = exchange(y.reshape(groups, rows, LANES))
    step = 32
    gate = pl.pallas_call(
        gate_kernel,
        grid=(rows // step,),
        in_specs=[pl.BlockSpec((step, z_in.shape[1]), lambda k: (k, 0))],
        out_specs=pl.BlockSpec((step, z_in.shape[1]), lambda k: (k, 0)),
        out_shape=jax.ShapeDtypeStruct(z_in.shape, F32),
        compiler_params=PARAMS,
        name="gate",
    )(z_in)
    return pl.pallas_call(
        norm_kernel,
        grid=(rows // step,),
        in_specs=[
            pl.BlockSpec((groups, step, LANES), lambda k: (0, k, 0)),
            pl.BlockSpec((step, z_in.shape[1]), lambda k: (k, 0)),
            full((1, z_in.shape[1])),
        ],
        out_specs=pl.BlockSpec((step, z_in.shape[1]), lambda k: (k, 0)),
        out_shape=jax.ShapeDtypeStruct(z_in.shape, BF16),
        scratch_shapes=[pltpu.VMEM((step, z_in.shape[1]), F32)],
        compiler_params=PARAMS,
        name="norm",
    )(y_tok, gate, norm_gain[None, :])


def solution(mesh):
    token = P(("ctx", "head"), None)
    in_specs = (
        token,
        token,
        token,
        token,
        P(None, "head"),
        P("head"),
        P(),
        P(),
        P("head"),
        P("head"),
        P("head"),
        P(),
    )
    return jax.shard_map(per_device, mesh=mesh, in_specs=in_specs, out_specs=token, check_vma=False)
```

```python
import jax
import jax.numpy as jnp
from jax import lax
from jax.experimental import pallas as pl
from jax.experimental.pallas import tpu as pltpu
from jax.sharding import PartitionSpec as P

BLOCK = 256
STATE = 128
WIDTH = 64
HEADS = 8
LANES = HEADS * WIDTH
PART = 256
RIM = 8
F32 = jnp.float32
BF16 = jnp.bfloat16


def silu(u):
    half = 0.5 * u
    return half + half * jnp.tanh(half)


def causal_conv(before, rows, taps, offset):
    count = rows.shape[0]
    padded = jnp.concatenate([before, rows.astype(F32)], 0)
    summed = offset + taps[0:1] * padded[RIM - 3 : RIM - 3 + count]
    summed = summed + taps[1:2] * padded[RIM - 2 : RIM - 2 + count]
    summed = summed + taps[2:3] * padded[RIM - 1 : RIM - 1 + count]
    summed = summed + taps[3:4] * padded[RIM : RIM + count]
    return silu(summed).astype(BF16)


def pack_kernel(x_ref, dt_ref, tail_ref, out_ref):
    rows = x_ref.shape[0]
    dt = dt_ref[...].astype(F32).T
    wide = LANES - 128
    row = lax.broadcasted_iota(jnp.int32, (RIM, wide), 0)
    for g in range(out_ref.shape[0]):
        start = LANES * g
        out_ref[g, :rows] = x_ref[:, start : start + LANES]
        tail = tail_ref[:, start : start + LANES].astype(F32)
        rest = jnp.concatenate([tail[:, wide:], jnp.zeros((RIM, wide - 128), F32)], 1)
        spare = jnp.where(row < 6, pltpu.roll(rest, 6, 0), 0.0)
        spare = jnp.where(row < 3, pltpu.roll(tail[:, :wide], 3, 0), spare)
        head = jnp.concatenate([dt[HEADS * g : HEADS * (g + 1)], jnp.zeros((HEADS, 128 - rows), F32)], 1)
        out_ref[g, rows:] = jnp.concatenate([head, spare], 1).astype(BF16)


def prep_kernel(g_ref, rim_ref, taps_ref, bias_ref, c_ref, bt_ref, carry):
    @pl.when(pl.program_id(0) == 0)
    def _():
        carry[...] = rim_ref[...].astype(F32)

    raw = g_ref[...]
    bcc = causal_conv(carry[...], raw, taps_ref[...], bias_ref[...])
    carry[...] = raw[BLOCK - RIM :].astype(F32)
    c_ref[...] = bcc[:, STATE:]
    bt_ref[...] = bcc[:, :STATE].astype(F32).T.astype(BF16)


def step_tables(dt_raw, par):
    shifted = dt_raw.astype(F32) + par[0]
    dt = jnp.maximum(shifted, 0.0) + jnp.log1p(jnp.exp(-jnp.abs(shifted)))
    cs = dt * -jnp.exp(par[1])
    lane = lax.broadcasted_iota(jnp.int32, cs.shape, 1) & (BLOCK - 1)
    step = 1
    while step < BLOCK:
        cs = cs + jnp.where(lane >= step, pltpu.roll(cs, step, 1), 0.0)
        step *= 2
    return cs, dt


def lane_pair(first, second, shape):
    lane = lax.broadcasted_iota(jnp.int32, shape, 1)
    return jnp.where(lane < WIDTH, first, second)


def state_kernel(
    x_ref, spare_ref, taps_ref, bias_ref, bt_ref, dt_ref, par_ref,
    xc_ref, local_ref, part_ref, rows_ref, carry, run
):
    @pl.when(pl.program_id(0) == 0)
    def _():
        spare = spare_ref[...].astype(F32)
        most = pltpu.roll(spare[:, 128:], 5, 0)
        rest = pltpu.roll(spare[:, 128:256], 2, 0)
        carry[...] = jnp.concatenate([most, rest], 1)
        run[...] = jnp.zeros_like(run)
        rows_ref[:HEADS], rows_ref[HEADS:] = step_tables(dt_ref[...], par_ref)

    here = pl.ds(pl.multiple_of(BLOCK * pl.program_id(0), BLOCK), BLOCK)
    cs = rows_ref[:HEADS, here]
    weight = jnp.exp(cs[:, BLOCK - 1 :] - cs) * rows_ref[HEADS:, here]
    raw = x_ref[...]
    xc = causal_conv(carry[...], raw, taps_ref[...], bias_ref[...])
    carry[...] = raw[BLOCK - RIM :].astype(F32)
    xc_ref[...] = xc
    local_ref[0] = run[...]
    bt = bt_ref[...].astype(F32)
    for pair in range(HEADS // 2):
        cols = slice(2 * WIDTH * pair, 2 * WIDTH * (pair + 1))
        parts, tots = [], []
        for h in (2 * pair, 2 * pair + 1):
            bw = (bt * weight[h : h + 1]).astype(BF16)
            parts.append(jnp.dot(bw, xc[:, cols], preferred_element_type=F32))
            tots.append(cs[h : h + 1, BLOCK - 1 :])
        tot = lane_pair(tots[0], tots[1], (1, 2 * WIDTH))
        st = lane_pair(parts[0], parts[1], (STATE, 2 * WIDTH))
        run[:STATE, cols] = run[:STATE, cols] * jnp.exp(tot) + st
        run[STATE:, cols] = run[STATE:, cols] + tot

    @pl.when(pl.program_id(0) == pl.num_programs(0) - 1)
    def _():
        part_ref[...] = jnp.zeros_like(part_ref)
        for i in range(STATE // 8):
            for j in range(LANES // PART):
                p = i * (LANES // PART) + j
                part_ref[p, :, :PART] = run[8 * i : 8 * (i + 1), PART * j : PART * (j + 1)]
                for half in range(PART // 128):
                    start = PART * j + 128 * half
                    part_ref[p, half : half + 1, PART:] = run[STATE : STATE + 1, start : start + 128]


def scan_kernel(part_ref, out_ref):
    run = jnp.zeros(out_ref.shape[1:], F32)
    for s in range(part_ref.shape[0]):
        out_ref[s] = run
        gain = jnp.concatenate([part_ref[s, half : half + 1, PART:] for half in range(PART // 128)], 1)
        run = run * jnp.exp(gain) + part_ref[s, :, :PART]


def diag_kernel(xc_ref, c_ref, bt_ref, rows_ref, skip_ref, y_ref):
    cs_t = rows_ref[:HEADS].T
    half = BLOCK // 2
    xc = xc_ref[...]
    scores = jnp.dot(c_ref[...], bt_ref[...], preferred_element_type=F32)
    for low, width in ((0, half), (half, BLOCK)):
        part = scores[low : low + half, :width]
        row = lax.broadcasted_iota(jnp.int32, (half, width), 0) + low
        col = lax.broadcasted_iota(jnp.int32, (half, width), 1)
        keep = row >= col
        for pair in range(HEADS // 2):
            cols = slice(2 * WIDTH * pair, 2 * WIDTH * (pair + 1))
            outs = []
            for h in (2 * pair, 2 * pair + 1):
                gap = cs_t[low : low + half, h : h + 1] - rows_ref[h : h + 1, :width]
                spread = jnp.exp(jnp.where(keep, gap, -1e30))
                m = (part * spread * rows_ref[8 + h : 9 + h, :width]).astype(BF16)
                outs.append(jnp.dot(m, xc[:width, cols], preferred_element_type=F32))
            y = lane_pair(outs[0], outs[1], (half, 2 * WIDTH))
            y_ref[low : low + half, cols] = (
                y + skip_ref[:, cols] * xc[low : low + half, cols].astype(F32)
            )


def join_kernel(diag_ref, c_ref, rows_ref, local_ref, in_ref, y_ref, entry):
    @pl.when(pl.program_id(0) == 0)
    def _():
        for i in range(STATE // 8):
            for j in range(LANES // PART):
                piece = in_ref[i * (LANES // PART) + j]
                entry[8 * i : 8 * (i + 1), PART * j : PART * (j + 1)] = piece

    hb = (entry[...] * jnp.exp(local_ref[0, STATE : STATE + 1]) + local_ref[0, :STATE]).astype(BF16)
    off = jnp.dot(c_ref[...], hb, preferred_element_type=F32)
    grow = jnp.exp(rows_ref[:HEADS]).T

    for pair in range(HEADS // 2):
        cols = slice(2 * WIDTH * pair, 2 * WIDTH * (pair + 1))
        h = 2 * pair
        scale = lane_pair(grow[:, h : h + 1], grow[:, h + 1 : h + 2], (BLOCK, 2 * WIDTH))
        y_ref[:, cols] = (diag_ref[:, cols] + off[:, cols] * scale).astype(BF16)


def gate_kernel(z_ref, out_ref):
    out_ref[...] = silu(z_ref[...].astype(F32))


def norm_kernel(y_ref, gate_ref, gain_ref, out_ref, gated_ref):
    groups = y_ref.shape[0]
    total = jnp.zeros((gate_ref.shape[0], 128), F32)
    for g in range(groups):
        at = slice(LANES * g, LANES * (g + 1))
        gated = y_ref[g].astype(F32) * gate_ref[:, at]
        gated_ref[:, at] = gated
        sq = gated * gated
        for start in range(0, LANES, 128):
            total = total + sq[:, start : start + 128]
    mean = jnp.sum(total, axis=1, keepdims=True) * (1.0 / (groups * LANES))
    out_ref[...] = (gated_ref[...] * lax.rsqrt(mean + 1e-05) * gain_ref[...]).astype(BF16)


def shift(value, axis, by):
    count = lax.axis_size(axis)
    return lax.ppermute(value, axis, [(i, i + by) for i in range(count - by)])


def held(value):
    return pltpu.with_memory_space_constraint(value, pltpu.HBM)


def full(shape):
    return pl.BlockSpec(shape, lambda k: tuple(0 for _ in shape))


def rows_of(width):
    return pl.BlockSpec((BLOCK, width), lambda k: (k, 0))


def lanes_of(height):
    return pl.BlockSpec((height, BLOCK), lambda k: (0, k))


WHOLE = pltpu.CompilerParams(vmem_limit_bytes=16 << 20)
PARAMS = pltpu.CompilerParams(dimension_semantics=("arbitrary",), vmem_limit_bytes=16 << 20)


def per_device(
    x_in, dt_raw, bc_in, z_in, conv_x, bias_x, conv_bc, bias_bc, dt_bias, a_log, d_skip, norm_gain
):
    groups = lax.axis_size("head")
    rows = x_in.shape[0]
    seg = rows * groups
    nblk = seg // BLOCK
    heads = dt_bias.shape[0]

    def exchange(value):
        return lax.all_to_all(value.transpose(1, 0, 2), "head", 1, 1, tiled=True).transpose(1, 0, 2)

    tail = shift(x_in[rows - RIM :], "ctx", 1)
    gathered = lax.all_gather(bc_in, "head", axis=0, tiled=True)
    tail, gathered = lax.optimization_barrier((tail, gathered))
    packed = pl.pallas_call(
        pack_kernel,
        out_shape=jax.ShapeDtypeStruct((groups, rows + RIM, LANES), BF16),
        compiler_params=WHOLE,
        name="pack",
    )(x_in, dt_raw, tail)
    first = exchange(packed)
    x_seg = first[:, :rows].reshape(seg, LANES)
    dt_seg = first[:, rows:, :rows].transpose(1, 0, 2).reshape(heads, seg)
    par = jnp.stack([dt_bias, a_log])[:, :, None]
    par = jnp.broadcast_to(par, (2, heads, seg))
    bc_rim = shift(gathered[seg - RIM :], "ctx", 1)
    c_mat, b_t = pl.pallas_call(
        prep_kernel,
        grid=(nblk,),
        in_specs=[
            rows_of(2 * STATE),
            full((RIM, 2 * STATE)),
            full((4, 2 * STATE)),
            full((1, 2 * STATE)),
        ],
        out_specs=[rows_of(STATE), lanes_of(STATE)],
        out_shape=[pltpu.HBM((seg, STATE), BF16), pltpu.HBM((STATE, seg), BF16)],
        scratch_shapes=[pltpu.VMEM((RIM, 2 * STATE), F32)],
        compiler_params=PARAMS,
        name="prep",
    )(gathered, bc_rim, conv_bc, bias_bc[None, :])
    pieces = (STATE // 8) * (LANES // PART)
    xc, local, parts, row_tab = pl.pallas_call(
        state_kernel,
        grid=(nblk,),
        in_specs=[
            rows_of(LANES),
            full((RIM, LANES)),
            full((4, LANES)),
            full((1, LANES)),
            lanes_of(STATE),
            full(dt_seg.shape),
            full(par.shape),
        ],
        out_specs=[
            rows_of(LANES),
            pl.BlockSpec((1, STATE + 8, LANES), lambda k: (k, 0, 0)),
            full((pieces, 8, PART + 128)),
            full((2 * heads, seg)),
        ],
        out_shape=[
            pltpu.HBM((seg, LANES), BF16),
            pltpu.HBM((nblk, STATE + 8, LANES), F32),
            jax.ShapeDtypeStruct((pieces, 8, PART + 128), F32),
            pltpu.HBM((2 * heads, seg), F32),
        ],
        scratch_shapes=[pltpu.VMEM((RIM, LANES), F32), pltpu.VMEM((STATE + 8, LANES), F32)],
        compiler_params=PARAMS,
        name="state",
    )(x_seg, first[groups - 1, rows:], conv_x, bias_x[None, :], held(b_t), dt_seg, par)
    c_mat, b_t, local, row_tab = [held(v) for v in (c_mat, b_t, local, row_tab)]
    skip = jnp.repeat(d_skip, WIDTH)[None, :]
    got = lax.all_to_all(parts, "ctx", 0, 0, tiled=True)
    before = pl.pallas_call(
        scan_kernel,
        out_shape=jax.ShapeDtypeStruct((pieces, 8, PART), F32),
        compiler_params=WHOLE,
        name="scan",
    )(got)
    incoming = lax.all_to_all(before, "ctx", 0, 0, tiled=True)
    y_diag = pl.pallas_call(
        diag_kernel,
        grid=(nblk,),
        in_specs=[
            rows_of(LANES),
            rows_of(STATE),
            lanes_of(STATE),
            lanes_of(2 * heads),
            full((1, LANES)),
        ],
        out_specs=rows_of(LANES),
        out_shape=pltpu.HBM((seg, LANES), F32),
        compiler_params=PARAMS,
        name="diag",
    )(held(xc), c_mat, b_t, row_tab, skip)
    y = pl.pallas_call(
        join_kernel,
        grid=(nblk,),
        in_specs=[
            rows_of(LANES),
            rows_of(STATE),
            lanes_of(2 * heads),
            pl.BlockSpec((1, STATE + 8, LANES), lambda k: (k, 0, 0)),
            full((pieces, 8, PART)),
        ],
        out_specs=rows_of(LANES),
        out_shape=pltpu.HBM((seg, LANES), BF16),
        scratch_shapes=[pltpu.VMEM((STATE, LANES), F32)],
        compiler_params=PARAMS,
        name="join",
    )(held(y_diag), c_mat, row_tab, local, incoming)
    y_tok = exchange(y.reshape(groups, rows, LANES))
    step = 32
    gate = pl.pallas_call(
        gate_kernel,
        grid=(rows // step,),
        in_specs=[pl.BlockSpec((step, z_in.shape[1]), lambda k: (k, 0))],
        out_specs=pl.BlockSpec((step, z_in.shape[1]), lambda k: (k, 0)),
        out_shape=jax.ShapeDtypeStruct(z_in.shape, F32),
        compiler_params=PARAMS,
        name="gate",
    )(z_in)
    return pl.pallas_call(
        norm_kernel,
        grid=(rows // step,),
        in_specs=[
            pl.BlockSpec((groups, step, LANES), lambda k: (0, k, 0)),
            pl.BlockSpec((step, z_in.shape[1]), lambda k: (k, 0)),
            full((1, z_in.shape[1])),
        ],
        out_specs=pl.BlockSpec((step, z_in.shape[1]), lambda k: (k, 0)),
        out_shape=jax.ShapeDtypeStruct(z_in.shape, BF16),
        scratch_shapes=[pltpu.VMEM((step, z_in.shape[1]), F32)],
        compiler_params=PARAMS,
        name="norm",
    )(y_tok, gate, norm_gain[None, :])


def solution(mesh):
    token = P(("ctx", "head"), None)
    in_specs = (
        token,
        token,
        token,
        token,
        P(None, "head"),
        P("head"),
        P(),
        P(),
        P("head"),
        P("head"),
        P("head"),
        P(),
    )
    return jax.shard_map(per_device, mesh=mesh, in_specs=in_specs, out_specs=token, check_vma=False)
```

```python
import jax
import jax.numpy as jnp
from jax import lax
from jax.experimental import pallas as pl
from jax.experimental.pallas import tpu as pltpu
from jax.sharding import PartitionSpec as P

BLOCK = 256
STATE = 128
WIDTH = 64
HEADS = 8
LANES = HEADS * WIDTH
PART = 256
RIM = 8
TWO = 2
F32 = jnp.float32
BF16 = jnp.bfloat16


def silu(u):
    half = 0.5 * u
    return half + half * jnp.tanh(half)


def causal_conv(before, rows, taps, offset):
    count = rows.shape[0]
    padded = jnp.concatenate([before, rows.astype(F32)], 0)
    summed = offset + taps[0:1] * padded[RIM - 3 : RIM - 3 + count]
    summed = summed + taps[1:2] * padded[RIM - 2 : RIM - 2 + count]
    summed = summed + taps[2:3] * padded[RIM - 1 : RIM - 1 + count]
    summed = summed + taps[3:4] * padded[RIM : RIM + count]
    return silu(summed).astype(BF16)


def pack_kernel(x_ref, dt_ref, tail_ref, out_ref):
    rows = x_ref.shape[0]
    dt = dt_ref[...].astype(F32).T
    wide = LANES - 128
    row = lax.broadcasted_iota(jnp.int32, (RIM, wide), 0)
    for g in range(out_ref.shape[0]):
        start = LANES * g
        out_ref[g, :rows] = x_ref[:, start : start + LANES]
        tail = tail_ref[:, start : start + LANES].astype(F32)
        rest = jnp.concatenate([tail[:, wide:], jnp.zeros((RIM, wide - 128), F32)], 1)
        spare = jnp.where(row < 6, pltpu.roll(rest, 6, 0), 0.0)
        spare = jnp.where(row < 3, pltpu.roll(tail[:, :wide], 3, 0), spare)
        head = jnp.concatenate([dt[HEADS * g : HEADS * (g + 1)], jnp.zeros((HEADS, 128 - rows), F32)], 1)
        out_ref[g, rows:] = jnp.concatenate([head, spare], 1).astype(BF16)


def prep_kernel(g_ref, rim_ref, taps_ref, bias_ref, c_ref, bt_ref, carry):
    @pl.when(pl.program_id(0) == 0)
    def _():
        carry[...] = rim_ref[...].astype(F32)

    raw = g_ref[...]
    bcc = causal_conv(carry[...], raw, taps_ref[...], bias_ref[...])
    carry[...] = raw[BLOCK - RIM :].astype(F32)
    c_ref[...] = bcc[:, STATE:]
    bt_ref[...] = bcc[:, :STATE].astype(F32).T.astype(BF16)


def step_tables(dt_raw, par):
    shifted = dt_raw.astype(F32) + par[0]
    dt = jnp.maximum(shifted, 0.0) + jnp.log1p(jnp.exp(-jnp.abs(shifted)))
    cs = dt * -jnp.exp(par[1])
    lane = lax.broadcasted_iota(jnp.int32, cs.shape, 1) & (BLOCK - 1)
    step = 1
    while step < BLOCK:
        cs = cs + jnp.where(lane >= step, pltpu.roll(cs, step, 1), 0.0)
        step *= 2
    return cs, dt


def lane_pair(first, second, shape):
    lane = lax.broadcasted_iota(jnp.int32, shape, 1)
    return jnp.where(lane < WIDTH, first, second)


def state_kernel(
    x_ref, spare_ref, taps_ref, bias_ref, bt_ref, dt_ref, par_ref,
    xc_ref, local_ref, part_ref, rows_ref, carry, run
):
    @pl.when(pl.program_id(0) == 0)
    def _():
        spare = spare_ref[...].astype(F32)
        most = pltpu.roll(spare[:, 128:], 5, 0)
        rest = pltpu.roll(spare[:, 128:256], 2, 0)
        carry[...] = jnp.concatenate([most, rest], 1)
        run[...] = jnp.zeros_like(run)
        rows_ref[:HEADS], rows_ref[HEADS:] = step_tables(dt_ref[...], par_ref)

    raw = x_ref[...]
    xc_all = causal_conv(carry[...], raw, taps_ref[...], bias_ref[...])
    carry[...] = raw[TWO * BLOCK - RIM :].astype(F32)
    xc_ref[...] = xc_all
    for sub in range(TWO):
        here = pl.ds(pl.multiple_of(BLOCK * (TWO * pl.program_id(0) + sub), BLOCK), BLOCK)
        inside = slice(BLOCK * sub, BLOCK * (sub + 1))
        cs = rows_ref[:HEADS, here]
        weight = jnp.exp(cs[:, BLOCK - 1 :] - cs) * rows_ref[HEADS:, here]
        xc = xc_all[inside]
        local_ref[sub] = run[...]
        bt = bt_ref[:, inside].astype(F32)
        for pair in range(HEADS // 2):
            cols = slice(2 * WIDTH * pair, 2 * WIDTH * (pair + 1))
            parts, tots = [], []
            for h in (2 * pair, 2 * pair + 1):
                bw = (bt * weight[h : h + 1]).astype(BF16)
                parts.append(jnp.dot(bw, xc[:, cols], preferred_element_type=F32))
                tots.append(cs[h : h + 1, BLOCK - 1 :])
            tot = lane_pair(tots[0], tots[1], (1, 2 * WIDTH))
            st = lane_pair(parts[0], parts[1], (STATE, 2 * WIDTH))
            run[:STATE, cols] = run[:STATE, cols] * jnp.exp(tot) + st
            run[STATE:, cols] = run[STATE:, cols] + tot

    @pl.when(pl.program_id(0) == pl.num_programs(0) - 1)
    def _():
        part_ref[...] = jnp.zeros_like(part_ref)
        for i in range(STATE // 8):
            for j in range(LANES // PART):
                p = i * (LANES // PART) + j
                part_ref[p, :, :PART] = run[8 * i : 8 * (i + 1), PART * j : PART * (j + 1)]
                for half in range(PART // 128):
                    start = PART * j + 128 * half
                    part_ref[p, half : half + 1, PART:] = run[STATE : STATE + 1, start : start + 128]


def scan_kernel(part_ref, out_ref):
    run = jnp.zeros(out_ref.shape[1:], F32)
    for s in range(part_ref.shape[0]):
        out_ref[s] = run
        gain = jnp.concatenate([part_ref[s, half : half + 1, PART:] for half in range(PART // 128)], 1)
        run = run * jnp.exp(gain) + part_ref[s, :, :PART]


def diag_kernel(xc_ref, c_ref, bt_ref, rows_ref, skip_ref, y_ref):
    cs_t = rows_ref[:HEADS].T
    half = BLOCK // 2
    xc = xc_ref[...]
    scores = jnp.dot(c_ref[...], bt_ref[...], preferred_element_type=F32)
    for low, width in ((0, half), (half, BLOCK)):
        part = scores[low : low + half, :width]
        row = lax.broadcasted_iota(jnp.int32, (half, width), 0) + low
        col = lax.broadcasted_iota(jnp.int32, (half, width), 1)
        keep = row >= col
        for pair in range(HEADS // 2):
            cols = slice(2 * WIDTH * pair, 2 * WIDTH * (pair + 1))
            outs = []
            for h in (2 * pair, 2 * pair + 1):
                gap = cs_t[low : low + half, h : h + 1] - rows_ref[h : h + 1, :width]
                spread = jnp.exp(jnp.where(keep, gap, -1e30))
                m = (part * spread * rows_ref[8 + h : 9 + h, :width]).astype(BF16)
                outs.append(jnp.dot(m, xc[:width, cols], preferred_element_type=F32))
            y = lane_pair(outs[0], outs[1], (half, 2 * WIDTH))
            y_ref[low : low + half, cols] = (
                y + skip_ref[:, cols] * xc[low : low + half, cols].astype(F32)
            )


def join_kernel(diag_ref, c_ref, rows_ref, local_ref, in_ref, y_ref, entry):
    @pl.when(pl.program_id(0) == 0)
    def _():
        for i in range(STATE // 8):
            for j in range(LANES // PART):
                piece = in_ref[i * (LANES // PART) + j]
                entry[8 * i : 8 * (i + 1), PART * j : PART * (j + 1)] = piece

    for sub in range(TWO):
        inside = slice(BLOCK * sub, BLOCK * (sub + 1))
        hb = (entry[...] * jnp.exp(local_ref[sub, STATE : STATE + 1]) + local_ref[sub, :STATE]).astype(BF16)
        off = jnp.dot(c_ref[inside], hb, preferred_element_type=F32)
        grow = jnp.exp(rows_ref[:HEADS, inside]).T
        for pair in range(HEADS // 2):
            cols = slice(2 * WIDTH * pair, 2 * WIDTH * (pair + 1))
            h = 2 * pair
            scale = lane_pair(grow[:, h : h + 1], grow[:, h + 1 : h + 2], (BLOCK, 2 * WIDTH))
            y_ref[inside, cols] = (diag_ref[inside, cols] + off[:, cols] * scale).astype(BF16)


def gate_kernel(z_ref, out_ref):
    out_ref[...] = silu(z_ref[...].astype(F32))


def norm_kernel(y_ref, gate_ref, gain_ref, out_ref, gated_ref):
    groups = y_ref.shape[0]
    total = jnp.zeros((gate_ref.shape[0], 128), F32)
    for g in range(groups):
        at = slice(LANES * g, LANES * (g + 1))
        gated = y_ref[g].astype(F32) * gate_ref[:, at]
        gated_ref[:, at] = gated
        sq = gated * gated
        for start in range(0, LANES, 128):
            total = total + sq[:, start : start + 128]
    mean = jnp.sum(total, axis=1, keepdims=True) * (1.0 / (groups * LANES))
    out_ref[...] = (gated_ref[...] * lax.rsqrt(mean + 1e-05) * gain_ref[...]).astype(BF16)


def shift(value, axis, by):
    count = lax.axis_size(axis)
    return lax.ppermute(value, axis, [(i, i + by) for i in range(count - by)])


def held(value):
    return pltpu.with_memory_space_constraint(value, pltpu.HBM)


def full(shape):
    return pl.BlockSpec(shape, lambda k: tuple(0 for _ in shape))


def rows_of(width, blocks=1):
    return pl.BlockSpec((blocks * BLOCK, width), lambda k: (k, 0))


def lanes_of(height, blocks=1):
    return pl.BlockSpec((height, blocks * BLOCK), lambda k: (0, k))


WHOLE = pltpu.CompilerParams(vmem_limit_bytes=16 << 20)
PARAMS = pltpu.CompilerParams(dimension_semantics=("arbitrary",), vmem_limit_bytes=16 << 20)


def per_device(
    x_in, dt_raw, bc_in, z_in, conv_x, bias_x, conv_bc, bias_bc, dt_bias, a_log, d_skip, norm_gain
):
    groups = lax.axis_size("head")
    rows = x_in.shape[0]
    seg = rows * groups
    nblk = seg // BLOCK
    heads = dt_bias.shape[0]

    def exchange(value):
        return lax.all_to_all(value.transpose(1, 0, 2), "head", 1, 1, tiled=True).transpose(1, 0, 2)

    tail = shift(x_in[rows - RIM :], "ctx", 1)
    gathered = lax.all_gather(bc_in, "head", axis=0, tiled=True)
    tail, gathered = lax.optimization_barrier((tail, gathered))
    packed = pl.pallas_call(
        pack_kernel,
        out_shape=jax.ShapeDtypeStruct((groups, rows + RIM, LANES), BF16),
        compiler_params=WHOLE,
        name="pack",
    )(x_in, dt_raw, tail)
    first = exchange(packed)
    x_seg = first[:, :rows].reshape(seg, LANES)
    dt_seg = first[:, rows:, :rows].transpose(1, 0, 2).reshape(heads, seg)
    par = jnp.stack([dt_bias, a_log])[:, :, None]
    par = jnp.broadcast_to(par, (2, heads, seg))
    bc_rim = shift(gathered[seg - RIM :], "ctx", 1)
    c_mat, b_t = pl.pallas_call(
        prep_kernel,
        grid=(nblk,),
        in_specs=[
            rows_of(2 * STATE),
            full((RIM, 2 * STATE)),
            full((4, 2 * STATE)),
            full((1, 2 * STATE)),
        ],
        out_specs=[rows_of(STATE), lanes_of(STATE)],
        out_shape=[pltpu.HBM((seg, STATE), BF16), pltpu.HBM((STATE, seg), BF16)],
        scratch_shapes=[pltpu.VMEM((RIM, 2 * STATE), F32)],
        compiler_params=PARAMS,
        name="prep",
    )(gathered, bc_rim, conv_bc, bias_bc[None, :])
    pieces = (STATE // 8) * (LANES // PART)
    xc, local, parts, row_tab = pl.pallas_call(
        state_kernel,
        grid=(nblk // TWO,),
        in_specs=[
            rows_of(LANES, TWO),
            full((RIM, LANES)),
            full((4, LANES)),
            full((1, LANES)),
            lanes_of(STATE, TWO),
            full(dt_seg.shape),
            full(par.shape),
        ],
        out_specs=[
            rows_of(LANES, TWO),
            pl.BlockSpec((TWO, STATE + 8, LANES), lambda k: (k, 0, 0)),
            full((pieces, 8, PART + 128)),
            full((2 * heads, seg)),
        ],
        out_shape=[
            pltpu.HBM((seg, LANES), BF16),
            pltpu.HBM((nblk, STATE + 8, LANES), F32),
            jax.ShapeDtypeStruct((pieces, 8, PART + 128), F32),
            pltpu.HBM((2 * heads, seg), F32),
        ],
        scratch_shapes=[pltpu.VMEM((RIM, LANES), F32), pltpu.VMEM((STATE + 8, LANES), F32)],
        compiler_params=PARAMS,
        name="state",
    )(x_seg, first[groups - 1, rows:], conv_x, bias_x[None, :], held(b_t), dt_seg, par)
    c_mat, b_t, local, row_tab = [held(v) for v in (c_mat, b_t, local, row_tab)]
    skip = jnp.repeat(d_skip, WIDTH)[None, :]
    got = lax.all_to_all(parts, "ctx", 0, 0, tiled=True)
    before = pl.pallas_call(
        scan_kernel,
        out_shape=jax.ShapeDtypeStruct((pieces, 8, PART), F32),
        compiler_params=WHOLE,
        name="scan",
    )(got)
    incoming = lax.all_to_all(before, "ctx", 0, 0, tiled=True)
    y_diag = pl.pallas_call(
        diag_kernel,
        grid=(nblk,),
        in_specs=[
            rows_of(LANES),
            rows_of(STATE),
            lanes_of(STATE),
            lanes_of(2 * heads),
            full((1, LANES)),
        ],
        out_specs=rows_of(LANES),
        out_shape=pltpu.HBM((seg, LANES), F32),
        compiler_params=PARAMS,
        name="diag",
    )(held(xc), c_mat, b_t, row_tab, skip)
    y = pl.pallas_call(
        join_kernel,
        grid=(nblk // TWO,),
        in_specs=[
            rows_of(LANES, TWO),
            rows_of(STATE, TWO),
            lanes_of(2 * heads, TWO),
            pl.BlockSpec((TWO, STATE + 8, LANES), lambda k: (k, 0, 0)),
            full((pieces, 8, PART)),
        ],
        out_specs=rows_of(LANES, TWO),
        out_shape=pltpu.HBM((seg, LANES), BF16),
        scratch_shapes=[pltpu.VMEM((STATE, LANES), F32)],
        compiler_params=PARAMS,
        name="join",
    )(held(y_diag), c_mat, row_tab, local, incoming)
    y_tok = exchange(y.reshape(groups, rows, LANES))
    step = 32
    gate = pl.pallas_call(
        gate_kernel,
        grid=(rows // step,),
        in_specs=[pl.BlockSpec((step, z_in.shape[1]), lambda k: (k, 0))],
        out_specs=pl.BlockSpec((step, z_in.shape[1]), lambda k: (k, 0)),
        out_shape=jax.ShapeDtypeStruct(z_in.shape, F32),
        compiler_params=PARAMS,
        name="gate",
    )(z_in)
    return pl.pallas_call(
        norm_kernel,
        grid=(rows // step,),
        in_specs=[
            pl.BlockSpec((groups, step, LANES), lambda k: (0, k, 0)),
            pl.BlockSpec((step, z_in.shape[1]), lambda k: (k, 0)),
            full((1, z_in.shape[1])),
        ],
        out_specs=pl.BlockSpec((step, z_in.shape[1]), lambda k: (k, 0)),
        out_shape=jax.ShapeDtypeStruct(z_in.shape, BF16),
        scratch_shapes=[pltpu.VMEM((step, z_in.shape[1]), F32)],
        compiler_params=PARAMS,
        name="norm",
    )(y_tok, gate, norm_gain[None, :])


def solution(mesh):
    token = P(("ctx", "head"), None)
    in_specs = (
        token,
        token,
        token,
        token,
        P(None, "head"),
        P("head"),
        P(),
        P(),
        P("head"),
        P("head"),
        P("head"),
        P(),
    )
    return jax.shard_map(per_device, mesh=mesh, in_specs=in_specs, out_specs=token, check_vma=False)
```
